512 devices in a mesh: len: 2 (over core), wid: 256 (over z, y, x).
Axes of the slice: x: 4, y: 8, z: 8, core: 2. Of those that a mesh axis runs over, the one named last changes fastest.
Arguments:
- latent: bfloat16 [4, 512, 128, 128], P('len', 'wid'), may hold values from -6 to 6
- offset: bfloat16 [4, 512, 3, 128], P('len', 'wid'), may hold values from 0 to 1
- occupied: int32 [4, 512, 128], P('len', 'wid'), may hold values 0 or 1
- pair_list: int32 [2, 256, 36], P('len', 'wid'), may hold values from -1 to 35, as said below
- w_send: bfloat16 [2, 128, 128], replicated, may hold values from -0.5 to 0.5
- w_recv: bfloat16 [2, 128, 128], replicated, may hold values from -0.5 to 0.5
- b_edge: float32 [2, 128], replicated, may hold values from -3 to 3
- w_disp: float32 [2, 3, 128], replicated, may hold values from -6 to 6
- w_dist: float32 [2, 128], replicated, may hold values from -6 to 6
- w_self: bfloat16 [2, 128, 128], replicated, may hold values from -0.5 to 0.5
- w_msg: bfloat16 [2, 128, 128], replicated, may hold values from -0.5 to 0.5
- b_node: float32 [2, 128], replicated, may hold values from -3 to 3
- w_out: bfloat16 [2, 128, 128], replicated, may hold values from -0.5 to 0.5
- gain: float32 [2, 128], replicated, may hold values from 0.5 to 1.5
Outputs:
- latent_out: bfloat16 [4, 512, 128, 128], P('len', 'wid')
The draws below stay inside these ranges and needn't reach their ends.
Inputs may be any that keep to these rules, and one draw needn't show every extreme that they name: `pair_list`: entry list of each device: distinct codes c * 9 + d with c < 4 and d < 9, all before the first -1, the rest -1. A device at an even index across the slope lists 36 or 18 codes; one at an odd index lists 36 // 4 or 4 codes (at least 1); device (0, 0) lists all 36.
All inputs are finite; a program needn't handle non-finite values. No bound on the sum of `occupied` on one device may be relied on, other than what follows from the above.
Results may differ from the reference program's by a relative error of at most 0.0023.
The reference program's roundings to bfloat16 on the way (of `send_proj`, `recv_proj`, `msg_in` and `node_hidden`) count: a program that leaves them out, or rounds other values in their place, can miss the bound.
Values may be sent and summed in bfloat16 or wider, within the bound.
A program may use at most 64 MiB of HBM per device.

```python
import jax
import jax.numpy as jnp
from jax import lax

H = 128
S = 128
CL = 2
CW = 2
STEPS = 2
PMAX = 36
NLC = 4
NWC = 512
N_LEN = 2
N_WID = 256


def draw_pair_list(key, part):
    devices_all = N_LEN * N_WID
    keys = jax.random.split(jax.random.fold_in(key, 17), 2)
    perms = jax.vmap(lambda sub: jax.random.permutation(sub, PMAX))(jax.random.split(keys[0], devices_all)).astype(jnp.int32)
    parity = jnp.arange(devices_all, dtype=jnp.int32) % N_WID % 2
    levels = jax.random.randint(keys[1], (devices_all,), 0, 2).astype(jnp.int32) + 2 * parity
    levels = levels.at[0].set(0)
    counts = jnp.maximum(jnp.right_shift(jnp.full((devices_all,), PMAX, jnp.int32), levels), 1)
    ranks = jnp.arange(PMAX, dtype=jnp.int32)[None, :]
    codes = jnp.where(ranks < counts[:, None], perms, -1)
    return codes.reshape(N_LEN, N_WID, PMAX).astype(jnp.int32)


def set_ends(drawn, own_key, low, high):
    spot = [jax.random.randint(jax.random.fold_in(own_key, axis), (), 0, length) for axis, length in enumerate(drawn.shape)]
    main_axis = drawn.shape.index(max(drawn.shape))
    neighbour = spot[:main_axis] + [(spot[main_axis] + 1) % drawn.shape[main_axis]] + spot[main_axis + 1:]
    return drawn.at[tuple(spot)].set(low).at[tuple(neighbour)].set(high)


def steps_of(stream_key, shape, shards, least, largest):
    loudness, own = 1.0, jax.random.fold_in(stream_key, 6)
    for position, blocks in shards:
        heights = jnp.exp(jax.random.uniform(jax.random.fold_in(own, position), (blocks,), jnp.float32, least / len(shards), largest / len(shards)))
        loudness = loudness * jnp.repeat(heights, shape[position] // blocks).reshape([-1 if axis == position else 1 for axis in range(len(shape))])
    return loudness


def noise(key, dims, scale, bound, cuts=(), kind=jnp.bfloat16):
    result = jax.random.normal(key, dims, jnp.float32) * scale
    if len(cuts) > 0:
        result = steps_of(key, dims, cuts, -0.22, 0.18) * result
    return jnp.clip(result, min=-bound, max=bound).astype(kind)


def setup_inputs(seed: int = 0) -> dict:
    splits = jax.random.split(jax.random.key(seed), 15)
    latent = noise(splits[0], (NLC, NWC, S, H), 1.0, 6.0, ((0, 2), (1, 256)))
    offset = jnp.clip(1.0 * jax.random.uniform(splits[1], (NLC, NWC, 3, S), jnp.float32) ** steps_of(splits[1], (NLC, NWC, 3, S), ((0, 2), (1, 256)), -0.2, 0.2), 0.0, 1.0).astype(jnp.bfloat16)
    occupied = set_ends((jax.random.randint(splits[2], (NLC, NWC, S), 0, 2) < 1).astype(jnp.int32), jax.random.fold_in(splits[2], 1), 0, 1)
    pair_list = draw_pair_list(jax.random.fold_in(splits[14], 71), 0)
    w_send = noise(splits[4], (STEPS, H, H), H ** -0.5, 0.5)
    w_recv = noise(splits[5], (STEPS, H, H), H ** -0.5, 0.5)
    b_edge = noise(splits[6], (STEPS, H), 0.5, 3.0, (), jnp.float32)
    w_disp = noise(splits[7], (STEPS, 3, H), 1.0, 6.0, (), jnp.float32)
    w_dist = noise(splits[8], (STEPS, H), 1.0, 6.0, (), jnp.float32)
    w_self = noise(splits[9], (STEPS, H, H), H ** -0.5, 0.5)
    w_msg = noise(splits[10], (STEPS, H, H), H ** -0.5, 0.5)
    b_node = noise(splits[11], (STEPS, H), 0.5, 3.0, (), jnp.float32)
    w_out = noise(splits[12], (STEPS, H, H), H ** -0.5, 0.5)
    gain = jnp.clip(1.0 + 0.1 * jax.random.normal(splits[13], (STEPS, H), jnp.float32), 0.5, 1.5)
    return {"latent": latent, "offset": offset, "occupied": occupied, "pair_list": pair_list, "w_send": w_send, "w_recv": w_recv, "b_edge": b_edge, "w_disp": w_disp, "w_dist": w_dist, "w_self": w_self, "w_msg": w_msg, "b_node": b_node, "w_out": w_out, "gain": gain}


EPSILON = 1e-05

def pair_tile(recv_rows, recv_geo, send_rows, send_geo, cell_shift, w_disp, w_dist):
    recv_off = recv_geo[:3]
    recv_occ = recv_geo[3]
    send_off = send_geo[:3] + cell_shift[:, None]
    send_occ = send_geo[3]
    recv_term = recv_rows.astype(jnp.float32) - jnp.einsum('cs,ch->sh', recv_off, w_disp, precision=lax.Precision.HIGHEST)
    send_term = send_rows.astype(jnp.float32) + jnp.einsum('cs,ch->sh', send_off, w_disp, precision=lax.Precision.HIGHEST)
    displace = send_off[:, None, :] - recv_off[:, :, None]
    dist_sq = lax.optimization_barrier(jnp.sum(displace * displace, axis=0))
    closeness = jnp.square(jnp.maximum(1.0 - dist_sq, 0.0)) * recv_occ[:, None] * send_occ[None, :]
    active = jnp.maximum(recv_term[:, None, :] + send_term[None, :, :] + dist_sq[:, :, None] * w_dist[None, None, :], 0.0)
    return lax.optimization_barrier(jnp.sum(active * closeness[:, :, None], axis=1))

def node_update(state, incoming, w_self, w_msg, b_node, w_out, gain):
    shape = state.shape
    width = shape[-1]
    agg_scale = shape[-2] / 8.0
    flat = state.reshape(-1, width)
    msg_in = (incoming.reshape(-1, width) / agg_scale).astype(jnp.bfloat16)
    pre = jnp.dot(flat, w_self, preferred_element_type=jnp.float32) + jnp.dot(msg_in, w_msg, preferred_element_type=jnp.float32) + b_node
    node_hidden = jnp.maximum(pre, 0.0).astype(jnp.bfloat16)
    node_out = jnp.dot(node_hidden, w_out, preferred_element_type=jnp.float32)
    center = lax.optimization_barrier(jnp.mean(node_out, axis=-1, keepdims=True))
    spread = lax.optimization_barrier(jnp.mean(jnp.square(node_out - center), axis=-1, keepdims=True))
    normed = (node_out - center) / jnp.sqrt(spread + EPSILON)
    return (flat.astype(jnp.float32) + normed * gain).astype(jnp.bfloat16).reshape(shape)

def pad_grid(field):
    wrapped = jnp.concatenate([field[:, -1:], field, field[:, :1]], axis=1)
    return jnp.pad(wrapped, [(1, 1)] + [(0, 0)] * (field.ndim - 1))

def reference(latent, offset, occupied, pair_list, w_send, w_recv, b_edge, w_disp, w_dist, w_self, w_msg, b_node, w_out, gain):
    width = latent.shape[-1]
    geometry = jnp.concatenate([offset.astype(jnp.float32), occupied.astype(jnp.float32)[:, :, None, :]], axis=2)
    padded_geo = pad_grid(geometry)
    pair_codes = pair_list.reshape(-1).astype(jnp.int32)
    device_ids = (jnp.arange(pair_codes.shape[0]) // PMAX).astype(jnp.int32)
    device_len = (device_ids // N_WID).astype(jnp.int32)
    device_wid = (device_ids % N_WID).astype(jnp.int32)
    state = latent
    for step in range(STEPS):
        flat = state.reshape(-1, width)
        send_proj = jnp.dot(flat, w_send[step], preferred_element_type=jnp.float32).astype(jnp.bfloat16).reshape(state.shape)
        recv_proj = (jnp.dot(flat, w_recv[step], preferred_element_type=jnp.float32) + b_edge[step]).astype(jnp.bfloat16).reshape(state.shape)
        padded_send = pad_grid(send_proj)
        disp_weights = w_disp[step]
        dist_weights = w_dist[step]

        def add_pair(incoming, item):
            code, dev_len, dev_wid = item
            safe = jnp.maximum(code, 0).astype(jnp.int32)
            cell = safe // 9
            direc = safe % 9
            row = (dev_len * CL + cell // CW).astype(jnp.int32)
            column = (dev_wid * CW + cell % CW).astype(jnp.int32)
            up_down = (direc // 3 - 1).astype(jnp.int32)
            sideways = (direc % 3 - 1).astype(jnp.int32)
            cell_shift = jnp.stack([up_down, sideways, jnp.zeros((), jnp.int32)]).astype(jnp.float32)

            def compute(operand):
                return pair_tile(recv_proj[row, column], geometry[row, column], padded_send[row + 1 + up_down, column + 1 + sideways], padded_geo[row + 1 + up_down, column + 1 + sideways], cell_shift, disp_weights, dist_weights)

            def skip(operand):
                return jnp.zeros((S, width), jnp.float32)
            tile = lax.cond(code >= 0, compute, skip, 0)
            return (incoming.at[row, column].add(tile), None)
        incoming, unused = lax.scan(add_pair, jnp.zeros(state.shape, jnp.float32), (pair_codes, device_len, device_wid))
        state = node_update(state, incoming, w_self[step], w_msg[step], b_node[step], w_out[step], gain[step])
    return state
```

```python
import functools

import jax
import jax.numpy as jnp
from jax import lax
from jax.experimental import pallas as pl
from jax.experimental.pallas import tpu as pltpu
from jax.sharding import PartitionSpec as P

EPSILON = 1e-05
FAR = 64.0
F32 = jnp.float32
BF16 = jnp.bfloat16
ROWS = 144
VMEM = pl.BlockSpec(memory_space=pltpu.VMEM)
SMEM = pl.BlockSpec(memory_space=pltpu.SMEM)


def iota(shape, dim):
    return lax.broadcasted_iota(jnp.int32, shape, dim)


def swap_lanes(x, step):
    if step == 64:
        return pltpu.roll(x, 64, 1)
    low = (iota(x.shape, 1) & step) == 0
    return jnp.where(low, pltpu.roll(x, 128 - step, 1), pltpu.roll(x, step, 1))


def pick_lanes(x, index):
    return jnp.take_along_axis(x, index, axis=1)


def split_row(row):
    index = 16 * iota((8, 128), 0) + (iota((8, 128), 1) & 15)
    return pick_lanes(jnp.broadcast_to(row, (8, 128)), index)


def split_rows(src, dst):
    lane = iota((8, 128), 1)
    for half in range(2):
        base = half * 64
        parts = [src[pl.ds(base + m, 8, stride=8), :] for m in range(8)]
        for bit in (4, 2, 1):
            step = 16 * bit
            low = (lane & step) == 0
            for m in range(8):
                if m & bit:
                    continue
                a, b = parts[m], parts[m + bit]
                parts[m] = jnp.where(low, a, pltpu.roll(b, step, 1))
                parts[m + bit] = jnp.where(low, pltpu.roll(a, 128 - step, 1), b)
        for q in range(8):
            dst[pl.ds(base + q, 8, stride=8), :] = parts[q]


def project(state, step, cell, w_send, w_recv, b_edge, w_disp, oi, msg, recv, flat, split):
    flat[...] = jnp.dot(state, w_send[step], preferred_element_type=F32)
    split_rows(flat, split)
    msg[cell, 0:128, :] = split[...].astype(BF16)
    r = jnp.dot(state, w_recv[step], preferred_element_type=F32) + b_edge[step : step + 1, :]
    r = r.astype(BF16).astype(F32)
    pull = sum(oi[cell, k] * w_disp[step, k : k + 1, :] for k in range(3))
    recv[cell] = r - pull


def prepare(latent, offset, occupied, w_send, w_recv, b_edge, w_disp, state, ranks, msg, recv, place, flat, split):
    upper = (iota((128, 128), 0) < iota((128, 128), 1)).astype(F32).astype(BF16)
    occ = occupied[...].astype(F32)
    before = jnp.dot(occ.astype(BF16), upper, preferred_element_type=F32)
    total = jnp.sum(occ, axis=1, keepdims=True)
    lane = iota((4, 128), 1).astype(F32)
    rank = jnp.where(occ > 0.5, before, total + lane - before)
    ranks[...] = rank
    slot = iota((128, 128), 0).astype(F32)
    for row in range(2):
        for col in range(2):
            given, cell = row * 2 + col, col * 2 + row
            perm = (slot == rank[given : given + 1, :]).astype(F32).astype(BF16)
            ordered = jnp.dot(perm, latent[given], preferred_element_type=F32).astype(BF16)
            state[cell] = ordered
            held = iota((128, 128), 0).astype(F32) < total[given : given + 1, :]
            for k in range(3):
                line = jnp.broadcast_to(offset[given, k : k + 1, :].astype(F32), (128, 128)).astype(BF16)
                spread = lax.dot_general(perm, line, (((1,), (1,)), ((), ())), preferred_element_type=F32)
                place[cell, k] = jnp.where(held, spread, -FAR) if k == 2 else spread
            geo = jnp.concatenate(
                [offset[given].astype(F32), occ[given : given + 1], jnp.zeros((12, 128), F32)], axis=0
            ).astype(BF16)
            moved = lax.dot_general(geo, perm, (((1,), (1,)), ((), ())), preferred_element_type=F32)
            msg[cell, 128:ROWS, :] = moved.astype(BF16)
            project(ordered, 0, cell, w_send, w_recv, b_edge, w_disp, place, msg, recv, flat, split)


def exchange(msg, grid, send_sem, recv_sem, own_sem):
    me_len, me_wid = lax.axis_index("len"), lax.axis_index("wid")
    count = lax.axis_size("wid")
    right, left = lax.rem(me_wid + 1, count), lax.rem(me_wid + count - 1, count)
    other = 1 - me_len
    barrier = pltpu.get_barrier_semaphore()
    for peer in ((me_len, left), (me_len, right), (other, me_wid), (other, left), (other, right)):
        pl.semaphore_signal(barrier, inc=1, device_id=peer, device_id_type=pl.DeviceIdType.MESH)
    own = pltpu.make_async_copy(msg, grid.at[pl.ds(0, 4)], own_sem)
    own.start()
    pl.semaphore_wait(barrier, 5)
    edge = 1 - me_len
    plan = (
        (pl.ds(0, 2), pl.ds(6, 2), (me_len, left)),
        (pl.ds(2, 2), pl.ds(4, 2), (me_len, right)),
        (pl.ds(edge, 1), pl.ds(11, 1), (other, left)),
        (pl.ds(2 + edge, 1), pl.ds(8, 1), (other, right)),
        (pl.ds(edge, 1), pl.ds(9, 1), (other, me_wid)),
        (pl.ds(2 + edge, 1), pl.ds(10, 1), (other, me_wid)),
    )
    copies = []
    for k, (src, dst, peer) in enumerate(plan):
        copy = pltpu.make_async_remote_copy(
            src_ref=msg.at[src],
            dst_ref=grid.at[dst],
            send_sem=send_sem.at[k],
            recv_sem=recv_sem.at[k],
            device_id=peer,
            device_id_type=pl.DeviceIdType.MESH,
        )
        copy.start()
        copies.append(copy)
    for copy in copies:
        copy.wait()
    own.wait()


def pairs(step, last, *refs):
    codes, grid, recv, place, state, ranks, w_send, w_recv, b_edge, w_disp, w_dist = refs[:11]
    w_self, w_msg, b_node, w_out, gain = refs[11:16]
    if last:
        (out,) = refs[16:17]
        rest = refs[17:]
    else:
        state_out, msg, recv_out = refs[16:19]
        rest = refs[19:]
    acc, floor, csum, sent, spots, near, counts, incoming, flat, split = rest
    me_len = lax.axis_index("len")

    for cell in range(12):
        geo = grid[cell, 128:ROWS, :].astype(F32)
        for k in range(3):
            row = geo[k : k + 1]
            if k == 2:
                row = row + FAR * (1.0 - geo[3:4])
            row = jnp.broadcast_to(row, (8, 128))
            index = 8 * iota((8, 128), 0) + (iota((8, 128), 1) >> 4)
            spots[cell, k, 0:8, :] = pick_lanes(row, index)
            spots[cell, k, 8:16, :] = pick_lanes(row, index + 64)
        counts[cell] = jnp.sum(geo[3:4]).astype(jnp.int32)

    acc[...] = jnp.zeros_like(acc)
    csum[...] = jnp.zeros_like(csum)

    def spread_recv(tile, _):
        cell, at = tile >> 4, pl.multiple_of((tile & 15) * 8, 8)
        x = -recv[cell, pl.ds(at, 8), :]
        for q in range(8):
            part = pick_lanes(x, 16 * q + (iota((8, 128), 1) & 15))
            floor[pl.ds(tile * 64 + q, 8, stride=8), :] = part
        return 0

    lax.fori_loop(0, 64, spread_recv, 0, unroll=2)

    push = [split_row(w_disp[step, k : k + 1, :]) for k in range(3)]
    pull = split_row(w_dist[step : step + 1, :])

    def one_pair(p, _):
        code = codes[p]
        safe = jnp.maximum(code, 0)
        given, direction = lax.div(safe, 9), lax.rem(safe, 9)
        row, col = given >> 1, given & 1
        up, side = lax.div(direction, 3) - 1, lax.rem(direction, 3) - 1
        cell = col * 2 + row
        at_row, at_col = row + 1 + up, col + 1 + side
        in_rows = (at_row == 1) | (at_row == 2)
        in_cols = (at_col == 1) | (at_col == 2)
        inside = in_rows & in_cols
        beyond = at_row == jnp.where(me_len == 0, 3, 0)
        source = jnp.where(
            inside,
            (at_col - 1) * 2 + at_row - 1,
            jnp.where(in_rows, jnp.where(at_col == 3, 6, 4) + at_row - 1, 8 + at_col),
        )
        live = (code >= 0) & (in_rows | beyond)

        @pl.when(live)
        def _():
            here, there = counts[cell], counts[source]
            shift = [jnp.full((1, 128), s.astype(F32)) for s in (up, side)]
            blocks = (there + 15) >> 4

            def fill(b, _):
                for r in range(2):
                    at = b * 2 + r
                    rows = pl.ds(pl.multiple_of(at * 8, 8), 8)
                    ox = spots[source, 0, pl.ds(at, 1), :] + shift[0]
                    oy = spots[source, 1, pl.ds(at, 1), :] + shift[1]
                    oz = spots[source, 2, pl.ds(at, 1), :]
                    s = grid[source, rows, :].astype(F32)
                    sent[rows, :] = s + ox * push[0] + oy * push[1] + oz * push[2]
                return 0

            lax.fori_loop(0, blocks, fill, 0)

            def block_of(ib, _):
                rows = [pl.ds(pl.multiple_of(ib * 16 + 8 * t, 8), 8) for t in range(2)]
                ox = [place[cell, 0, rows[t], :] - shift[0] for t in range(2)]
                oy = [place[cell, 1, rows[t], :] - shift[1] for t in range(2)]
                oz = [place[cell, 2, rows[t], :] for t in range(2)]
                first = pl.multiple_of((cell * 128 + ib * 16) * 8, 128)
                nr = [floor[pl.ds(first + 8 * i, 8), :] for i in range(16)]

                def closeness(b):
                    made = []
                    for r in range(2):
                        at = b * 2 + r
                        x = spots[source, 0, pl.ds(at, 1), :]
                        y = spots[source, 1, pl.ds(at, 1), :]
                        z = spots[source, 2, pl.ds(at, 1), :]
                        for t in range(2):
                            dx, dy, dz = ox[t] - x, oy[t] - y, oz[t] - z
                            d = dx * dx + dy * dy + dz * dz
                            c = jnp.maximum(1.0 - d, 0.0)
                            made.append((d, c * c))
                    return made

                def put(slot, made):
                    for k, (d, c) in enumerate(made):
                        near[pl.ds(pl.multiple_of(slot * 64 + 8 * k, 8), 8), :] = d
                        near[pl.ds(pl.multiple_of(slot * 64 + 32 + 8 * k, 8), 8), :] = c

                put(0, closeness(0))

                def senders(b, carry):
                    total, weight = list(carry[:16]), list(carry[16:])
                    slot = b & 1
                    base = slot * 64
                    follow = closeness(jnp.minimum(b + 1, 7))
                    for r in range(2):
                        s = sent[pl.ds(pl.multiple_of((b * 2 + r) * 8, 8), 8), :]
                        for i in range(16):
                            line = 16 * r + i
                            d = near[pl.ds(base + line, 1), :]
                            c = near[pl.ds(base + 32 + line, 1), :]
                            total[i] = total[i] + c * jnp.maximum(s + d * pull, nr[i])
                        for t in range(2):
                            own = pl.ds(pl.multiple_of(base + 32 + 16 * r + 8 * t, 8), 8)
                            weight[t] = weight[t] + near[own, :]
                    put(1 - slot, follow)
                    return tuple(total) + tuple(weight)

                at = pl.multiple_of(cell * 128 + ib * 16, 16)
                carry = [acc[pl.ds(first + 8 * i, 8), :] for i in range(16)]
                carry += [csum[pl.ds(at + 8 * t, 8), :] for t in range(2)]
                carry = lax.fori_loop(0, blocks, senders, tuple(carry))
                for i in range(16):
                    acc[pl.ds(first + 8 * i, 8), :] = carry[i]
                for t in range(2):
                    csum[pl.ds(at + 8 * t, 8), :] = carry[16 + t]
                return 0

            lax.fori_loop(0, (here + 15) >> 4, block_of, 0)

        return 0

    lax.fori_loop(0, codes.shape[0], one_pair, 0)

    def gather(tile, _):
        cell, at = tile >> 4, pl.multiple_of((tile & 15) * 8, 8)
        lane = iota((8, 128), 1)
        parts = [acc[pl.ds(tile * 64 + q, 8, stride=8), :] for q in range(8)]
        for bit in (4, 2, 1):
            low = (lane & (16 * bit)) == 0
            parts = [
                jnp.where(low, parts[q], parts[q + bit])
                + swap_lanes(jnp.where(low, parts[q + bit], parts[q]), 16 * bit)
                for q in range(bit)
            ]
        weight = jnp.sum(csum[pl.ds(pl.multiple_of(tile * 8, 8), 8), :], axis=1, keepdims=True) * (1.0 / 16.0)
        incoming[cell, pl.ds(at, 8), :] = parts[0] + recv[cell, pl.ds(at, 8), :] * weight
        return 0

    lax.fori_loop(0, 64, gather, 0, unroll=2)

    for cell in range(4):
        h = state[cell]
        msg_in = (incoming[cell] * (8.0 / 128.0)).astype(BF16)
        pre = (
            jnp.dot(h, w_self[step], preferred_element_type=F32)
            + jnp.dot(msg_in, w_msg[step], preferred_element_type=F32)
            + b_node[step : step + 1, :]
        )
        hidden = jnp.maximum(pre, 0.0).astype(BF16)
        y = jnp.dot(hidden, w_out[step], preferred_element_type=F32)
        center = jnp.mean(y, axis=-1, keepdims=True)
        spread = jnp.mean(jnp.square(y - center), axis=-1, keepdims=True)
        normed = (y - center) / jnp.sqrt(spread + EPSILON)
        new = (h.astype(F32) + normed * gain[step : step + 1, :]).astype(BF16)
        if last:
            given = (cell & 1) * 2 + (cell >> 1)
            slot = iota((128, 128), 0).astype(F32)
            perm = (slot == ranks[given : given + 1, :]).astype(F32).astype(BF16)
            back = lax.dot_general(perm, new, (((0,), (0,)), ((), ())), preferred_element_type=F32)
            out[given] = back.astype(BF16)
        else:
            state_out[cell] = new
            msg[cell, 128:ROWS, :] = grid[cell, 128:ROWS, :]
            project(new, 1, cell, w_send, w_recv, b_edge, w_disp, place, msg, recv_out, flat, split)


def per_device(
    latent, offset, occupied, pair_list, w_send, w_recv, b_edge, w_disp, w_dist, w_self, w_msg, b_node, w_out, gain
):
    shape = jax.ShapeDtypeStruct
    state, ranks, msg, recv, place = pl.pallas_call(
        prepare,
        name="prepare",
        out_shape=(
            shape((4, 128, 128), BF16),
            shape((4, 128), F32),
            shape((4, ROWS, 128), BF16),
            shape((4, 128, 128), F32),
            shape((4, 3, 128, 128), F32),
        ),
        in_specs=[VMEM] * 7,
        out_specs=(VMEM,) * 5,
        scratch_shapes=[pltpu.VMEM((128, 128), F32)] * 2,
    )(
        latent.reshape(4, 128, 128),
        offset.reshape(4, 3, 128),
        occupied.reshape(4, 128),
        w_send,
        w_recv,
        b_edge,
        w_disp,
    )
    swap = pl.pallas_call(
        exchange,
        name="exchange",
        out_shape=shape((12, ROWS, 128), BF16),
        in_specs=[VMEM],
        out_specs=VMEM,
        scratch_shapes=[pltpu.SemaphoreType.DMA((6,)), pltpu.SemaphoreType.DMA((6,)), pltpu.SemaphoreType.DMA],
        compiler_params=pltpu.CompilerParams(collective_id=0, has_side_effects=True),
    )
    codes = pair_list.reshape(-1)
    for step in range(2):
        last = step == 1
        grid = swap(msg)
        if last:
            out_shape = shape((4, 128, 128), BF16)
            out_specs = VMEM
        else:
            out_shape = (shape((4, 128, 128), BF16), shape((4, ROWS, 128), BF16), shape((4, 128, 128), F32))
            out_specs = (VMEM,) * 3
        made = pl.pallas_call(
            functools.partial(pairs, step, last),
            name=f"pairs_{step}",
            out_shape=out_shape,
            in_specs=[SMEM] + [VMEM] * 15,
            out_specs=out_specs,
            scratch_shapes=[
                pltpu.VMEM((4096, 128), F32),
                pltpu.VMEM((4096, 128), F32),
                pltpu.VMEM((512, 128), F32),
                pltpu.VMEM((128, 128), F32),
                pltpu.VMEM((12, 3, 16, 128), F32),
                pltpu.VMEM((128, 128), F32),
                pltpu.SMEM((12,), jnp.int32),
                pltpu.VMEM((4, 128, 128), F32),
                pltpu.VMEM((128, 128), F32),
                pltpu.VMEM((128, 128), F32),
            ],
        )(
            codes, grid, recv, place, state, ranks, w_send, w_recv, b_edge, w_disp, w_dist, w_self, w_msg, b_node,
            w_out, gain,
        )
        if not last:
            state, msg, recv = made
    return made.reshape(latent.shape)


def solution(mesh):
    return jax.shard_map(
        per_device,
        mesh=mesh,
        in_specs=(
            P("len", "wid", None, None),
            P("len", "wid", None, None),
            P("len", "wid", None),
            P("len", "wid", None),
        )
        + (P(),) * 10,
        out_specs=P("len", "wid", None, None),
        check_vma=False,
    )
```

```python
import functools

import jax
import jax.numpy as jnp
from jax import lax
from jax.experimental import pallas as pl
from jax.experimental.pallas import tpu as pltpu
from jax.sharding import PartitionSpec as P

EPSILON = 1e-05
FAR = 64.0
F32 = jnp.float32
BF16 = jnp.bfloat16
ROWS = 144
VMEM = pl.BlockSpec(memory_space=pltpu.VMEM)
SMEM = pl.BlockSpec(memory_space=pltpu.SMEM)


def iota(shape, dim):
    return lax.broadcasted_iota(jnp.int32, shape, dim)


def swap_lanes(x, step):
    if step == 64:
        return pltpu.roll(x, 64, 1)
    low = (iota(x.shape, 1) & step) == 0
    return jnp.where(low, pltpu.roll(x, 128 - step, 1), pltpu.roll(x, step, 1))


def pick_lanes(x, index):
    return jnp.take_along_axis(x, index, axis=1)


def split_row(row):
    index = 16 * iota((8, 128), 0) + (iota((8, 128), 1) & 15)
    return pick_lanes(jnp.broadcast_to(row, (8, 128)), index)


def split_rows(src, dst):
    lane = iota((8, 128), 1)
    for base in range(0, src.shape[0], 64):
        parts = [src[pl.ds(base + m, 8, stride=8), :] for m in range(8)]
        for bit in (4, 2, 1):
            step = 16 * bit
            low = (lane & step) == 0
            for m in range(8):
                if m & bit:
                    continue
                a, b = parts[m], parts[m + bit]
                parts[m] = jnp.where(low, a, pltpu.roll(b, step, 1))
                parts[m + bit] = jnp.where(low, pltpu.roll(a, 128 - step, 1), b)
        for q in range(8):
            dst[pl.ds(base + q, 8, stride=8), :] = parts[q]


def project(state, step, w_send, w_recv, b_edge, w_disp, place, msg, recv, flat, split):
    flat[...] = jnp.dot(state, w_send[step], preferred_element_type=F32)
    split_rows(flat, split)
    r = jnp.dot(state, w_recv[step], preferred_element_type=F32) + b_edge[step : step + 1, :]
    r = r.astype(BF16).astype(F32)
    for cell in range(4):
        here = slice(cell * 128, cell * 128 + 128)
        msg[cell, 0:128, :] = split[here, :].astype(BF16)
        pull = sum(place[cell, k] * w_disp[step, k : k + 1, :] for k in range(3))
        recv[cell] = r[here] - pull


def prepare(latent, offset, occupied, w_send, w_recv, b_edge, w_disp, state, ranks, msg, recv, place, flat, split):
    upper = (iota((128, 128), 0) < iota((128, 128), 1)).astype(F32).astype(BF16)
    occ = occupied[...].astype(F32)
    before = jnp.dot(occ.astype(BF16), upper, preferred_element_type=F32)
    total = jnp.sum(occ, axis=1, keepdims=True)
    lane = iota((4, 128), 1).astype(F32)
    rank = jnp.where(occ > 0.5, before, total + lane - before)
    ranks[...] = rank
    slot = iota((128, 128), 0).astype(F32)
    for row in range(2):
        for col in range(2):
            given, cell = row * 2 + col, col * 2 + row
            perm = (slot == rank[given : given + 1, :]).astype(F32).astype(BF16)
            ordered = jnp.dot(perm, latent[given], preferred_element_type=F32).astype(BF16)
            state[cell] = ordered
            held = iota((128, 128), 0).astype(F32) < total[given : given + 1, :]
            for k in range(3):
                line = jnp.broadcast_to(offset[given, k : k + 1, :].astype(F32), (128, 128)).astype(BF16)
                spread = lax.dot_general(perm, line, (((1,), (1,)), ((), ())), preferred_element_type=F32)
                place[cell, k] = jnp.where(held, spread, -FAR) if k == 2 else spread
            geo = jnp.concatenate(
                [offset[given].astype(F32), occ[given : given + 1], jnp.zeros((12, 128), F32)], axis=0
            ).astype(BF16)
            moved = lax.dot_general(geo, perm, (((1,), (1,)), ((), ())), preferred_element_type=F32)
            msg[cell, 128:ROWS, :] = moved.astype(BF16)
    project(state[...].reshape(512, 128), 0, w_send, w_recv, b_edge, w_disp, place, msg, recv, flat, split)


def exchange(msg, grid, send_sem, recv_sem, own_sem):
    me_len, me_wid = lax.axis_index("len"), lax.axis_index("wid")
    count = lax.axis_size("wid")
    right, left = lax.rem(me_wid + 1, count), lax.rem(me_wid + count - 1, count)
    other = 1 - me_len
    barrier = pltpu.get_barrier_semaphore()
    for peer in ((me_len, left), (me_len, right), (other, me_wid), (other, left), (other, right)):
        pl.semaphore_signal(barrier, inc=1, device_id=peer, device_id_type=pl.DeviceIdType.MESH)
    own = pltpu.make_async_copy(msg, grid.at[pl.ds(0, 4)], own_sem)
    own.start()
    pl.semaphore_wait(barrier, 5)
    edge = 1 - me_len
    plan = (
        (pl.ds(0, 2), pl.ds(6, 2), (me_len, left)),
        (pl.ds(2, 2), pl.ds(4, 2), (me_len, right)),
        (pl.ds(edge, 1), pl.ds(11, 1), (other, left)),
        (pl.ds(2 + edge, 1), pl.ds(8, 1), (other, right)),
        (pl.ds(edge, 1), pl.ds(9, 1), (other, me_wid)),
        (pl.ds(2 + edge, 1), pl.ds(10, 1), (other, me_wid)),
    )
    copies = []
    for k, (src, dst, peer) in enumerate(plan):
        copy = pltpu.make_async_remote_copy(
            src_ref=msg.at[src],
            dst_ref=grid.at[dst],
            send_sem=send_sem.at[k],
            recv_sem=recv_sem.at[k],
            device_id=peer,
            device_id_type=pl.DeviceIdType.MESH,
        )
        copy.start()
        copies.append(copy)
    for copy in copies:
        copy.wait()
    own.wait()


def pairs(step, last, *refs):
    codes, grid, recv, place, state, ranks, w_send, w_recv, b_edge, w_disp, w_dist = refs[:11]
    w_self, w_msg, b_node, w_out, gain = refs[11:16]
    if last:
        (out,) = refs[16:17]
        rest = refs[17:]
    else:
        state_out, msg, recv_out = refs[16:19]
        rest = refs[19:]
    acc, floor, csum, sent, spots, far, close, counts, incoming, flat, split = rest
    me_len = lax.axis_index("len")

    for cell in range(12):
        geo = grid[cell, 128:ROWS, :].astype(F32)
        for k in range(3):
            row = geo[k : k + 1]
            if k == 2:
                row = row + FAR * (1.0 - geo[3:4])
            row = jnp.broadcast_to(row, (8, 128))
            index = 8 * iota((8, 128), 0) + (iota((8, 128), 1) >> 4)
            spots[cell, k, 0:8, :] = pick_lanes(row, index)
            spots[cell, k, 8:16, :] = pick_lanes(row, index + 64)
        counts[cell] = jnp.sum(geo[3:4]).astype(jnp.int32)

    acc[...] = jnp.zeros_like(acc)
    csum[...] = jnp.zeros_like(csum)
    incoming[...] = jnp.zeros_like(incoming)

    for cell in range(4):

        def spread_recv(group, _, cell=cell):
            for t in range(4):
                at = pl.multiple_of(group * 32 + 8 * t, 8)
                x = -recv[cell, pl.ds(at, 8), :]
                for q in range(8):
                    part = pick_lanes(x, 16 * q + (iota((8, 128), 1) & 15))
                    floor[pl.ds((cell * 128 + at) * 8 + q, 8, stride=8), :] = part
            return 0

        lax.fori_loop(0, (counts[cell] + 31) >> 5, spread_recv, 0)

    push = [split_row(w_disp[step, k : k + 1, :]) for k in range(3)]
    pull = split_row(w_dist[step : step + 1, :])

    def one_pair(p, _):
        code = codes[p]
        given = (code * 57) >> 9
        direction = code - given * 9
        row, col = given >> 1, given & 1
        high = (direction * 11) >> 5
        up, side = high - 1, direction - high * 3 - 1
        cell = col * 2 + row
        at_row, at_col = row + 1 + up, col + 1 + side
        in_rows = (at_row == 1) | (at_row == 2)
        in_cols = (at_col == 1) | (at_col == 2)
        beyond = at_row == jnp.where(me_len == 0, 3, 0)
        source = jnp.where(
            in_rows & in_cols,
            (at_col - 1) * 2 + at_row - 1,
            jnp.where(in_rows, jnp.where(at_col == 3, 6, 4) + at_row - 1, 8 + at_col),
        )

        @pl.when(in_rows | beyond)
        def _():
            here, there = counts[cell], counts[source]
            shift = [jnp.full((1, 128), s.astype(F32)) for s in (up, side)]
            lines = (there + 7) >> 3

            def fill(b, _):
                for r in range(4):
                    at = b * 4 + r
                    rows = pl.ds(pl.multiple_of(at * 8, 8), 8)
                    ox = spots[source, 0, pl.ds(at, 1), :] + shift[0]
                    oy = spots[source, 1, pl.ds(at, 1), :] + shift[1]
                    oz = spots[source, 2, pl.ds(at, 1), :]
                    s = grid[source, rows, :].astype(F32)
                    sent[rows, :] = s + ox * push[0] + oy * push[1] + oz * push[2]
                return 0

            lax.fori_loop(0, (lines + 3) >> 2, fill, 0)

            def block_of(tiles, tile, _):
                many = 8 * tiles
                start = pl.multiple_of(cell * 128 + tile * 8, 8)
                rows = [pl.ds(pl.multiple_of(tile * 8 + 8 * t, 8), 8) for t in range(tiles)]
                ox = [place[cell, 0, rows[t], :] - shift[0] for t in range(tiles)]
                oy = [place[cell, 1, rows[t], :] - shift[1] for t in range(tiles)]
                oz = [place[cell, 2, rows[t], :] for t in range(tiles)]

                def measure(b, weight):
                    weight = list(weight)
                    for r in range(4):
                        at = b * 4 + r
                        x = spots[source, 0, pl.ds(at, 1), :]
                        y = spots[source, 1, pl.ds(at, 1), :]
                        z = spots[source, 2, pl.ds(at, 1), :]
                        for t in range(tiles):
                            dx, dy, dz = ox[t] - x, oy[t] - y, oz[t] - z
                            d = dx * dx + dy * dy + dz * dz
                            c = jnp.maximum(1.0 - d, 0.0)
                            c = c * c
                            put = pl.ds(pl.multiple_of(at * 16 + 8 * t, 8), 8)
                            far[put, :] = d
                            close[put, :] = c
                            weight[t] = weight[t] + c
                    return tuple(weight)

                weight = tuple(csum[pl.ds(start + 8 * t, 8), :] for t in range(tiles))
                weight = lax.fori_loop(0, (lines + 3) >> 2, measure, weight)
                for t in range(tiles):
                    csum[pl.ds(start + 8 * t, 8), :] = weight[t]

                first = pl.multiple_of(start * 8, 64)
                nr = [floor[pl.ds(first + 8 * i, 8), :] for i in range(many)]

                def senders(width, at, carry):
                    total = list(carry)
                    for r in range(width):
                        s = sent[pl.ds(pl.multiple_of((at + r) * 8, 8), 8), :]
                        for i in range(many):
                            d = far[pl.ds((at + r) * 16 + i, 1), :]
                            c = close[pl.ds((at + r) * 16 + i, 1), :]
                            total[i] = total[i] + c * jnp.maximum(s + d * pull, nr[i])
                    return tuple(total)

                total = tuple(acc[pl.ds(first + 8 * i, 8), :] for i in range(many))
                total = lax.fori_loop(0, lines >> 1, lambda b, c: senders(2, 2 * b, c), total)
                total = lax.fori_loop(lines & ~1, lines, lambda b, c: senders(1, b, c), total)
                for i in range(many):
                    acc[pl.ds(first + 8 * i, 8), :] = total[i]
                return 0

            wide = (here + 7) >> 3
            lax.fori_loop(0, wide >> 1, lambda b, c: block_of(2, 2 * b, c), 0)
            lax.fori_loop(wide & ~1, wide, lambda b, c: block_of(1, b, c), 0)

        return 0

    listed = sum((codes[p] >= 0).astype(jnp.int32) for p in range(codes.shape[0]))
    lax.fori_loop(0, listed, one_pair, 0)

    for cell in range(4):

        def gather(group, _, cell=cell):
            lane = iota((8, 128), 1)
            for t in range(4):
                at = pl.multiple_of(group * 32 + 8 * t, 8)
                base = (cell * 128 + at) * 8
                parts = [acc[pl.ds(base + q, 8, stride=8), :] for q in range(8)]
                for bit in (4, 2, 1):
                    low = (lane & (16 * bit)) == 0
                    parts = [
                        jnp.where(low, parts[q], parts[q + bit])
                        + swap_lanes(jnp.where(low, parts[q + bit], parts[q]), 16 * bit)
                        for q in range(bit)
                    ]
                weight = jnp.sum(csum[pl.ds(cell * 128 + at, 8), :], axis=1, keepdims=True) * (1.0 / 16.0)
                incoming[pl.ds(cell * 128 + at, 8), :] = parts[0] + recv[cell, pl.ds(at, 8), :] * weight
            return 0

        lax.fori_loop(0, (counts[cell] + 31) >> 5, gather, 0)

    h = state[...].reshape(512, 128)
    msg_in = (incoming[...] * (8.0 / 128.0)).astype(BF16)
    pre = (
        jnp.dot(h, w_self[step], preferred_element_type=F32)
        + jnp.dot(msg_in, w_msg[step], preferred_element_type=F32)
        + b_node[step : step + 1, :]
    )
    hidden = jnp.maximum(pre, 0.0).astype(BF16)
    y = jnp.dot(hidden, w_out[step], preferred_element_type=F32)
    center = jnp.mean(y, axis=-1, keepdims=True)
    spread = jnp.mean(jnp.square(y - center), axis=-1, keepdims=True)
    normed = (y - center) / jnp.sqrt(spread + EPSILON)
    new = (h.astype(F32) + normed * gain[step : step + 1, :]).astype(BF16)
    if last:
        slot = iota((128, 128), 0).astype(F32)
        for cell in range(4):
            given = (cell & 1) * 2 + (cell >> 1)
            perm = (slot == ranks[given : given + 1, :]).astype(F32).astype(BF16)
            here = new[cell * 128 : cell * 128 + 128]
            back = lax.dot_general(perm, here, (((0,), (0,)), ((), ())), preferred_element_type=F32)
            out[given] = back.astype(BF16)
    else:
        state_out[...] = new.reshape(4, 128, 128)
        for cell in range(4):
            msg[cell, 128:ROWS, :] = grid[cell, 128:ROWS, :]
        project(new, 1, w_send, w_recv, b_edge, w_disp, place, msg, recv_out, flat, split)


def per_device(
    latent, offset, occupied, pair_list, w_send, w_recv, b_edge, w_disp, w_dist, w_self, w_msg, b_node, w_out, gain
):
    shape = jax.ShapeDtypeStruct
    state, ranks, msg, recv, place = pl.pallas_call(
        prepare,
        name="prepare",
        out_shape=(
            shape((4, 128, 128), BF16),
            shape((4, 128), F32),
            shape((4, ROWS, 128), BF16),
            shape((4, 128, 128), F32),
            shape((4, 3, 128, 128), F32),
        ),
        in_specs=[VMEM] * 7,
        out_specs=(VMEM,) * 5,
        scratch_shapes=[pltpu.VMEM((512, 128), F32)] * 2,
    )(
        latent.reshape(4, 128, 128),
        offset.reshape(4, 3, 128),
        occupied.reshape(4, 128),
        w_send,
        w_recv,
        b_edge,
        w_disp,
    )
    swap = pl.pallas_call(
        exchange,
        name="exchange",
        out_shape=shape((12, ROWS, 128), BF16),
        in_specs=[VMEM],
        out_specs=VMEM,
        scratch_shapes=[pltpu.SemaphoreType.DMA((6,)), pltpu.SemaphoreType.DMA((6,)), pltpu.SemaphoreType.DMA],
        compiler_params=pltpu.CompilerParams(collective_id=0, has_side_effects=True),
    )
    codes = pair_list.reshape(-1)
    for step in range(2):
        last = step == 1
        grid = swap(msg)
        if last:
            out_shape = shape((4, 128, 128), BF16)
            out_specs = VMEM
        else:
            out_shape = (shape((4, 128, 128), BF16), shape((4, ROWS, 128), BF16), shape((4, 128, 128), F32))
            out_specs = (VMEM,) * 3
        made = pl.pallas_call(
            functools.partial(pairs, step, last),
            name=f"pairs_{step}",
            out_shape=out_shape,
            in_specs=[SMEM] + [VMEM] * 15,
            out_specs=out_specs,
            scratch_shapes=[
                pltpu.VMEM((4096, 128), F32),
                pltpu.VMEM((4096, 128), F32),
                pltpu.VMEM((512, 128), F32),
                pltpu.VMEM((128, 128), F32),
                pltpu.VMEM((12, 3, 16, 128), F32),
                pltpu.VMEM((256, 128), F32),
                pltpu.VMEM((256, 128), F32),
                pltpu.SMEM((12,), jnp.int32),
                pltpu.VMEM((512, 128), F32),
                pltpu.VMEM((512, 128), F32),
                pltpu.VMEM((512, 128), F32),
            ],
        )(
            codes, grid, recv, place, state, ranks, w_send, w_recv, b_edge, w_disp, w_dist, w_self, w_msg, b_node,
            w_out, gain,
        )
        if not last:
            state, msg, recv = made
    return made.reshape(latent.shape)


def solution(mesh):
    return jax.shard_map(
        per_device,
        mesh=mesh,
        in_specs=(
            P("len", "wid", None, None),
            P("len", "wid", None, None),
            P("len", "wid", None),
            P("len", "wid", None),
        )
        + (P(),) * 10,
        out_specs=P("len", "wid", None, None),
        check_vma=False,
    )
```

```python
import functools

import jax
import jax.numpy as jnp
from jax import lax
from jax.experimental import pallas as pl
from jax.experimental.pallas import tpu as pltpu
from jax.sharding import PartitionSpec as P

EPSILON = 1e-05
FAR = 64.0
F32 = jnp.float32
BF16 = jnp.bfloat16
ROWS = 144
LIMIT = 16 << 20
VMEM = pl.BlockSpec(memory_space=pltpu.VMEM)
FIXED = pl.BlockSpec(memory_space=pltpu.HBM)
SMEM = pl.BlockSpec(memory_space=pltpu.SMEM)


def iota(shape, dim):
    return lax.broadcasted_iota(jnp.int32, shape, dim)


def swap_lanes(x, step):
    if step == 64:
        return pltpu.roll(x, 64, 1)
    low = (iota(x.shape, 1) & step) == 0
    return jnp.where(low, pltpu.roll(x, 128 - step, 1), pltpu.roll(x, step, 1))


def pick_lanes(x, index):
    return jnp.take_along_axis(x, index, axis=1)


def split_row(row):
    index = 16 * iota((8, 128), 0) + (iota((8, 128), 1) & 15)
    return pick_lanes(jnp.broadcast_to(row, (8, 128)), index)


def split_rows(src, dst):
    lane = iota((8, 128), 1)
    for base in range(0, src.shape[0], 64):
        parts = [src[pl.ds(base + m, 8, stride=8), :] for m in range(8)]
        for bit in (4, 2, 1):
            step = 16 * bit
            low = (lane & step) == 0
            for m in range(8):
                if m & bit:
                    continue
                a, b = parts[m], parts[m + bit]
                parts[m] = jnp.where(low, a, pltpu.roll(b, step, 1))
                parts[m + bit] = jnp.where(low, pltpu.roll(a, 128 - step, 1), b)
        for q in range(8):
            dst[pl.ds(base + q, 8, stride=8), :] = parts[q]


def project_send(state, step, w_send, msg, flat, split):
    flat[...] = jnp.dot(state, w_send[step], preferred_element_type=F32)
    split_rows(flat, split)
    for cell in range(4):
        msg[cell, 0:128, :] = split[cell * 128 : cell * 128 + 128, :].astype(BF16)


def project_recv(state, step, w_recv, b_edge, w_disp, place, recv):
    r = jnp.dot(state, w_recv[step], preferred_element_type=F32) + b_edge[step : step + 1, :]
    r = r.astype(BF16).astype(F32)
    for cell in range(4):
        pull = sum(place[cell, k] * w_disp[k, step : step + 1, :] for k in range(3))
        recv[cell] = r[cell * 128 : cell * 128 + 128] - pull


def peers():
    me_len, me_wid = lax.axis_index("len"), lax.axis_index("wid")
    count = lax.axis_size("wid")
    right, left = lax.rem(me_wid + 1, count), lax.rem(me_wid + count - 1, count)
    return me_len, me_wid, left, right


def greet():
    me_len, me_wid, left, right = peers()
    other = 1 - me_len
    barrier = pltpu.get_barrier_semaphore()
    for peer in ((me_len, left), (me_len, right), (other, me_wid), (other, left), (other, right)):
        pl.semaphore_signal(barrier, inc=1, device_id=peer, device_id_type=pl.DeviceIdType.MESH)


def send_all(msg, grid, send_sem, recv_sem, own_sem):
    me_len, me_wid, left, right = peers()
    other = 1 - me_len
    edge = 1 - me_len
    pl.semaphore_wait(pltpu.get_barrier_semaphore(), 5)
    plan = (
        (pl.ds(0, 2), pl.ds(6, 2), (me_len, left)),
        (pl.ds(2, 2), pl.ds(4, 2), (me_len, right)),
        (pl.ds(edge, 1), pl.ds(11, 1), (other, left)),
        (pl.ds(2 + edge, 1), pl.ds(8, 1), (other, right)),
        (pl.ds(edge, 1), pl.ds(9, 1), (other, me_wid)),
        (pl.ds(2 + edge, 1), pl.ds(10, 1), (other, me_wid)),
    )
    copies = []
    for k, (src, dst, peer) in enumerate(plan):
        copy = pltpu.make_async_remote_copy(
            src_ref=msg.at[src],
            dst_ref=grid.at[dst],
            send_sem=send_sem.at[k],
            recv_sem=recv_sem.at[k],
            device_id=peer,
            device_id_type=pl.DeviceIdType.MESH,
        )
        copy.start()
        copies.append(copy)
    own = pltpu.make_async_copy(msg, grid.at[pl.ds(0, 4)], own_sem)
    own.start()
    return copies + [own]


def begin(latent_in, offset, occupied, w_send_in, w_recv_in, b_edge, w_disp, *refs):
    state, ranks, recv, place, grid, table, msg, flat, split, send_sem, recv_sem, own_sem = refs[:12]
    latent, w_send, w_recv, load_sem = refs[12:]
    greet()
    loads = [
        pltpu.make_async_copy(src, dst, load_sem.at[k])
        for k, (src, dst) in enumerate(((latent_in, latent), (w_send_in, w_send), (w_recv_in, w_recv)))
    ]
    for load in loads:
        load.start()
    occ = occupied[...].astype(F32)
    total = jnp.sum(occ, axis=1, keepdims=True)
    line, lane = iota((128, 128), 0), iota((128, 128), 1)
    slot = line.astype(F32)
    same = (line == lane).astype(F32).astype(BF16)
    both = (((1,), (1,)), ((), ()))
    perms = [None] * 4
    for row in range(2):
        for col in range(2):
            given, cell = row * 2 + col, col * 2 + row
            held = occ[given : given + 1]
            key = (offset[row, 1, col : col + 1, :].astype(F32) + 2.0 * (1.0 - held)).astype(BF16)
            key_row = jnp.broadcast_to(key.astype(F32), (128, 128))
            key_col = lax.dot_general(same, key_row.astype(BF16), both, preferred_element_type=F32)
            ahead = (key_col < key_row) | ((key_col == key_row) & (line < lane))
            rank = jnp.sum(ahead.astype(F32), axis=0, keepdims=True)
            ranks[given : given + 1, :] = rank
            perm = (slot == rank).astype(F32).astype(BF16)
            perms[cell] = perm
            full = slot < total[given : given + 1, :]
            for k in range(3):
                part = jnp.broadcast_to(offset[row, k, col : col + 1, :].astype(F32), (128, 128)).astype(BF16)
                spread = lax.dot_general(perm, part, both, preferred_element_type=F32)
                place[cell, k] = jnp.where(full, spread, -FAR) if k == 2 else spread
            geo = [offset[row, k, col : col + 1, :].astype(F32) for k in range(3)]
            geo = jnp.concatenate(geo + [held, jnp.zeros((12, 128), F32)], axis=0).astype(BF16)
            moved = lax.dot_general(geo, perm, both, preferred_element_type=F32)
            msg[cell, 128:ROWS, :] = moved.astype(BF16)
    for load in loads:
        load.wait()
    for cell in range(4):
        given = (cell & 1) * 2 + (cell >> 1)
        state[cell] = jnp.dot(perms[cell], latent[given], preferred_element_type=F32).astype(BF16)
    project_send(state[...].reshape(512, 128), 0, w_send, msg, flat, split)
    project_recv(state[...].reshape(512, 128), 0, w_recv, b_edge, w_disp, place, recv)
    for copy in send_all(msg, grid, send_sem, recv_sem, own_sem):
        copy.wait()
    wide_lane = iota((1, 128), 1)
    step = (wide_lane * 8) & 127
    tall = iota((16, 128), 0)
    table_lane = iota((64, 128), 1)
    tops, bottoms = [], []
    for cell in range(4):
        given = (cell & 1) * 2 + (cell >> 1)
        inside = (tall * 8 + 7).astype(F32) < total[given : given + 1, :]
        tops.append(jnp.where(inside, place[cell, 1, pl.ds(7, 16, stride=8), :], 2.0))
        bottoms.append(place[cell, 1, pl.ds(0, 16, stride=8), :])
    top, bottom = jnp.concatenate(tops, axis=0), jnp.concatenate(bottoms, axis=0)
    high, low = jnp.zeros((64, 128), F32), jnp.zeros((64, 128), F32)
    held = jnp.zeros((1, 128), F32)
    for cell in range(12):
        geo = grid[cell, 128:ROWS, :].astype(F32)
        count = jnp.sum(geo[3:4], axis=1, keepdims=True)
        mine = table_lane == cell
        held = jnp.where(wide_lane == cell, count, held)
        at = (wide_lane * 8).astype(F32)
        begins = pick_lanes(jnp.broadcast_to(geo[1:2], (8, 128)), jnp.broadcast_to(step, (8, 128)))[0:1]
        ends = pick_lanes(jnp.broadcast_to(geo[1:2], (8, 128)), jnp.broadcast_to(step + 7, (8, 128)))[0:1]
        begins = jnp.where(at < count, begins, 4.0)
        ends = jnp.where(at + 7.0 < count, ends, 4.0)
        high = jnp.where(mine, jnp.sum((begins < top).astype(F32), axis=1, keepdims=True), high)
        low = jnp.where(mine, jnp.sum((ends <= bottom).astype(F32), axis=1, keepdims=True), low)
    table[0:64, :] = high.astype(jnp.int32)
    table[64:128, :] = low.astype(jnp.int32)
    table[128:136, :] = jnp.broadcast_to(held, (8, 128)).astype(jnp.int32)


def node_update(step, state, msg_in, w_self, w_msg, b_node, w_out, gain):
    h = state[...].reshape(512, 128)
    pre = (
        jnp.dot(h, w_self[step], preferred_element_type=F32)
        + jnp.dot(msg_in, w_msg[step], preferred_element_type=F32)
        + b_node[step : step + 1, :]
    )
    hidden = jnp.maximum(pre, 0.0).astype(BF16)
    y = jnp.dot(hidden, w_out[step], preferred_element_type=F32)
    center = jnp.mean(y, axis=-1, keepdims=True)
    spread = jnp.mean(jnp.square(y - center), axis=-1, keepdims=True)
    normed = (y - center) / jnp.sqrt(spread + EPSILON)
    return (h.astype(F32) + normed * gain[step : step + 1, :]).astype(BF16)


def middle(state, msg_in, before, place, w_send, w_recv, b_edge, w_disp, *refs):
    w_self, w_msg, b_node, w_out, gain = refs[:5]
    state_out, recv, grid, msg, flat, split, send_sem, recv_sem, own_sem = refs[5:]
    greet()
    new = node_update(0, state, msg_in[...], w_self, w_msg, b_node, w_out, gain)
    state_out[...] = new.reshape(4, 128, 128)
    for cell in range(4):
        msg[cell, 128:ROWS, :] = before[cell, 128:ROWS, :]
    project_send(new, 1, w_send, msg, flat, split)
    project_recv(new, 1, w_recv, b_edge, w_disp, place, recv)
    for copy in send_all(msg, grid, send_sem, recv_sem, own_sem):
        copy.wait()


def pairs(step, last, codes, table, grid, recv, place, w_disp, w_dist, *refs):
    if last:
        state, ranks, w_self, w_msg, b_node, w_out, gain, out = refs[:8]
        rest = refs[8:]
    else:
        (msg_in,) = refs[:1]
        rest = refs[1:]
    acc, floor, csum, sent, queue, spots, far, close, incoming, plan, many = rest
    me_len = lax.axis_index("len")
    counts = [table[128, cell] for cell in range(4)]

    for cell in range(12):
        geo = grid[cell, 128:ROWS, :].astype(F32)
        for k in range(3):
            row = geo[k : k + 1]
            if k == 2:
                row = row + FAR * (1.0 - geo[3:4])
            row = jnp.broadcast_to(row, (8, 128))
            index = 8 * iota((8, 128), 0) + (iota((8, 128), 1) >> 4)
            spots[cell, k, 0:8, :] = pick_lanes(row, index)
            spots[cell, k, 8:16, :] = pick_lanes(row, index + 64)
            spots[cell, k, 16:24, :] = jnp.full((8, 128), FAR)

    acc[...] = jnp.zeros_like(acc)
    csum[...] = jnp.zeros_like(csum)
    incoming[...] = jnp.zeros_like(incoming)

    for cell in range(4):

        def spread_recv(group, _, cell=cell):
            for t in range(4):
                at = pl.multiple_of(group * 32 + 8 * t, 8)
                x = -recv[cell, pl.ds(at, 8), :]
                for q in range(8):
                    part = pick_lanes(x, 16 * q + (iota((8, 128), 1) & 15))
                    floor[pl.ds((cell * 128 + at) * 8 + q, 8, stride=8), :] = part
            return 0

        lax.fori_loop(0, (counts[cell] + 31) >> 5, spread_recv, 0)

    push = [split_row(w_disp[k, step : step + 1, :]) for k in range(3)]
    pull = split_row(w_dist[step : step + 1, :])

    for cell in range(4):
        many[cell] = 0

    def enlist(p, _):
        code = codes[p]
        given = (code * 57) >> 9
        direction = code - given * 9
        row, col = given >> 1, given & 1
        high = (direction * 11) >> 5
        up, side = high - 1, direction - high * 3 - 1
        cell = col * 2 + row
        at_row, at_col = row + 1 + up, col + 1 + side
        in_rows = (at_row == 1) | (at_row == 2)
        in_cols = (at_col == 1) | (at_col == 2)
        beyond = at_row == jnp.where(me_len == 0, 3, 0)
        source = jnp.where(
            in_rows & in_cols,
            (at_col - 1) * 2 + at_row - 1,
            jnp.where(in_rows, jnp.where(at_col == 3, 6, 4) + at_row - 1, 8 + at_col),
        )

        @pl.when(in_rows | beyond)
        def _():
            spot = many[cell]
            plan[cell, 3 * spot] = source
            plan[cell, 3 * spot + 1] = up
            plan[cell, 3 * spot + 2] = side
            many[cell] = spot + 1

        return 0

    listed = sum((codes[p] >= 0).astype(jnp.int32) for p in range(codes.shape[0]))
    lax.fori_loop(0, listed, enlist, 0)

    def one_cell(cell, _):
        here, entries = table[128, cell], many[cell]

        def fill(q, _):
            source, up, side = (plan[cell, 3 * q + k] for k in range(3))
            shift = [jnp.full((1, 128), s.astype(F32)) for s in (up, side)]

            def some(b, _):
                for r in range(4):
                    at = b * 4 + r
                    ox = spots[source, 0, pl.ds(at, 1), :] + shift[0]
                    oy = spots[source, 1, pl.ds(at, 1), :] + shift[1]
                    oz = spots[source, 2, pl.ds(at, 1), :]
                    s = grid[source, pl.ds(pl.multiple_of(at * 8, 8), 8), :].astype(F32)
                    put = pl.ds(pl.multiple_of(q * 160 + at * 8, 8), 8)
                    sent[put, :] = s + ox * push[0] + oy * push[1] + oz * push[2]
                return 0

            return lax.fori_loop(0, (table[128, source] + 31) >> 5, some, 0)

        lax.fori_loop(0, entries, fill, 0)

        def block_of(tiles, tile):
            size = 8 * tiles
            start = pl.multiple_of(cell * 128 + tile * 8, 8)
            rows = [pl.ds(pl.multiple_of(tile * 8 + 8 * t, 8), 8) for t in range(tiles)]
            place_x = [place[cell, 0, rows[t], :] for t in range(tiles)]
            place_y = [place[cell, 1, rows[t], :] for t in range(tiles)]
            oz = [place[cell, 2, rows[t], :] for t in range(tiles)]

            def measure(q, carry):
                front, weight = carry[0], carry[1:]
                source, up, side = (plan[cell, 3 * q + k] for k in range(3))
                lines = (table[128, source] + 7) >> 3
                most = jnp.where(side == 1, table[cell * 16 + tile + tiles - 1, source], lines)
                least = jnp.where(side == -1, table[64 + cell * 16 + tile, source], 0)
                span = jnp.maximum(most - least, 0)
                ox = [x - up.astype(F32) for x in place_x]
                oy = [y - side.astype(F32) for y in place_y]

                def some(b, weight):
                    weight = list(weight)
                    for r in range(4):
                        at, to = least + b * 4 + r, front + b * 4 + r
                        x = spots[source, 0, pl.ds(at, 1), :]
                        y = spots[source, 1, pl.ds(at, 1), :]
                        z = spots[source, 2, pl.ds(at, 1), :]
                        take = pl.ds(pl.multiple_of(q * 160 + at * 8, 8), 8)
                        queue[pl.ds(pl.multiple_of(to * 8, 8), 8), :] = sent[take, :]
                        for t in range(tiles):
                            dx, dy, dz = ox[t] - x, oy[t] - y, oz[t] - z
                            d = dx * dx + dy * dy + dz * dz
                            c = jnp.maximum(1.0 - d, 0.0)
                            c = c * c
                            put = pl.ds(pl.multiple_of(to * 16 + 8 * t, 8), 8)
                            far[put, :] = d
                            close[put, :] = c
                            weight[t] = weight[t] + c
                    return tuple(weight)

                weight = lax.fori_loop(0, (span + 3) >> 2, some, weight)
                return (front + span,) + tuple(weight)

            nothing = jnp.zeros((8, 128), F32)
            carry = lax.fori_loop(0, entries, measure, (jnp.int32(0),) + (nothing,) * tiles)
            front = carry[0]
            for t in range(tiles):
                csum[pl.ds(start + 8 * t, 8), :] = carry[1 + t]
            for r in range(3):
                queue[pl.ds(pl.multiple_of((front + r) * 8, 8), 8), :] = nothing
                for t in range(tiles):
                    far[pl.ds(pl.multiple_of((front + r) * 16 + 8 * t, 8), 8), :] = nothing
                    close[pl.ds(pl.multiple_of((front + r) * 16 + 8 * t, 8), 8), :] = nothing

            first = pl.multiple_of(start * 8, 64)
            nr = [floor[pl.ds(first + 8 * i, 8), :] for i in range(size)]

            def senders(b, carry):
                sums = list(carry)
                for r in range(4):
                    at = b * 4 + r
                    s = queue[pl.ds(pl.multiple_of(at * 8, 8), 8), :]
                    for i in range(size):
                        d = far[pl.ds(at * 16 + i, 1), :]
                        c = close[pl.ds(at * 16 + i, 1), :]
                        sums[i] = sums[i] + c * jnp.maximum(s + d * pull, nr[i])
                return tuple(sums)

            sums = lax.fori_loop(0, (front + 3) >> 2, senders, (nothing,) * size)
            for i in range(size):
                acc[pl.ds(first + 8 * i, 8), :] = sums[i]

        def pair_of_tiles(b, _):
            block_of(2, 2 * b)
            return 0

        def odd_tile(b, _):
            block_of(1, b)
            return 0

        tiles = (here + 7) >> 3
        lax.fori_loop(0, tiles >> 1, pair_of_tiles, 0)
        lax.fori_loop(tiles & ~1, tiles, odd_tile, 0)
        return 0

    lax.fori_loop(0, 4, one_cell, 0)

    for cell in range(4):

        def gather(group, _, cell=cell):
            lane = iota((8, 128), 1)
            for t in range(4):
                at = pl.multiple_of(group * 32 + 8 * t, 8)
                base = (cell * 128 + at) * 8
                parts = [acc[pl.ds(base + q, 8, stride=8), :] for q in range(8)]
                for bit in (4, 2, 1):
                    low = (lane & (16 * bit)) == 0
                    parts = [
                        jnp.where(low, parts[q], parts[q + bit])
                        + swap_lanes(jnp.where(low, parts[q + bit], parts[q]), 16 * bit)
                        for q in range(bit)
                    ]
                weight = jnp.sum(csum[pl.ds(cell * 128 + at, 8), :], axis=1, keepdims=True) * (1.0 / 16.0)
                incoming[pl.ds(cell * 128 + at, 8), :] = parts[0] + recv[cell, pl.ds(at, 8), :] * weight
            return 0

        lax.fori_loop(0, (counts[cell] + 31) >> 5, gather, 0)

    rounded = (incoming[...] * (8.0 / 128.0)).astype(BF16)
    if not last:
        msg_in[...] = rounded
        return
    new = node_update(step, state, rounded, w_self, w_msg, b_node, w_out, gain)
    slot = iota((128, 128), 0).astype(F32)
    for cell in range(4):
        given = (cell & 1) * 2 + (cell >> 1)
        perm = (slot == ranks[given : given + 1, :]).astype(F32).astype(BF16)
        here = new[cell * 128 : cell * 128 + 128]
        back = lax.dot_general(perm, here, (((0,), (0,)), ((), ())), preferred_element_type=F32)
        out[given] = back.astype(BF16)


def per_device(
    latent, offset, occupied, pair_list, w_send, w_recv, b_edge, w_disp, w_dist, w_self, w_msg, b_node, w_out, gain
):
    shape = jax.ShapeDtypeStruct
    w_disp = w_disp.transpose(1, 0, 2)
    sems = [pltpu.SemaphoreType.DMA((6,)), pltpu.SemaphoreType.DMA((6,)), pltpu.SemaphoreType.DMA]
    work = [pltpu.VMEM((4, ROWS, 128), BF16), pltpu.VMEM((512, 128), F32), pltpu.VMEM((512, 128), F32)]
    cells, wide = shape((4, 128, 128), BF16), shape((4, 128, 128), F32)
    state, ranks, recv, place, grid, table = pl.pallas_call(
        begin,
        name="begin",
        out_shape=(
            cells,
            shape((4, 128), F32),
            wide,
            shape((4, 3, 128, 128), F32),
            shape((12, ROWS, 128), BF16),
            shape((136, 128), jnp.int32),
        ),
        in_specs=[FIXED, VMEM, VMEM, FIXED, FIXED, VMEM, VMEM],
        out_specs=(VMEM,) * 6,
        scratch_shapes=work
        + sems
        + [pltpu.VMEM((4, 128, 128), BF16), pltpu.VMEM((2, 128, 128), BF16), pltpu.VMEM((2, 128, 128), BF16)]
        + [pltpu.SemaphoreType.DMA((3,))],
        compiler_params=pltpu.CompilerParams(collective_id=0, has_side_effects=True, vmem_limit_bytes=LIMIT),
    )(
        latent.reshape(4, 128, 128),
        offset.transpose(0, 2, 1, 3),
        occupied.reshape(4, 128),
        w_send,
        w_recv,
        b_edge,
        w_disp,
    )
    codes = pair_list.reshape(-1)
    scratch = [
        pltpu.VMEM((4096, 128), F32),
        pltpu.VMEM((4096, 128), F32),
        pltpu.VMEM((512, 128), F32),
        pltpu.VMEM((9 * 160, 128), F32),
        pltpu.VMEM((148 * 8, 128), F32),
        pltpu.VMEM((12, 3, 24, 128), F32),
        pltpu.VMEM((148 * 16, 128), F32),
        pltpu.VMEM((148 * 16, 128), F32),
        pltpu.VMEM((512, 128), F32),
        pltpu.SMEM((4, 27), jnp.int32),
        pltpu.SMEM((4,), jnp.int32),
    ]
    msg_in = pl.pallas_call(
        functools.partial(pairs, 0, False),
        name="pairs_0",
        out_shape=shape((512, 128), BF16),
        in_specs=[SMEM] * 2 + [VMEM] * 5,
        out_specs=VMEM,
        scratch_shapes=scratch,
        compiler_params=pltpu.CompilerParams(vmem_limit_bytes=LIMIT),
    )(codes, table, grid, recv, place, w_disp, w_dist)
    state, recv, grid = pl.pallas_call(
        middle,
        name="middle",
        out_shape=(cells, wide, shape((12, ROWS, 128), BF16)),
        in_specs=[VMEM] * 13,
        out_specs=(VMEM,) * 3,
        scratch_shapes=work + sems,
        compiler_params=pltpu.CompilerParams(collective_id=1, has_side_effects=True, vmem_limit_bytes=LIMIT),
    )(state, msg_in, grid, place, w_send, w_recv, b_edge, w_disp, w_self, w_msg, b_node, w_out, gain)
    out = pl.pallas_call(
        functools.partial(pairs, 1, True),
        name="pairs_1",
        out_shape=cells,
        in_specs=[SMEM] * 2 + [VMEM] * 12,
        out_specs=VMEM,
        scratch_shapes=scratch,
        compiler_params=pltpu.CompilerParams(vmem_limit_bytes=LIMIT),
    )(codes, table, grid, recv, place, w_disp, w_dist, state, ranks, w_self, w_msg, b_node, w_out, gain)
    return out.reshape(latent.shape)


def solution(mesh):
    return jax.shard_map(
        per_device,
        mesh=mesh,
        in_specs=(
            P("len", "wid", None, None),
            P("len", "wid", None, None),
            P("len", "wid", None),
            P("len", "wid", None),
        )
        + (P(),) * 10,
        out_specs=P("len", "wid", None, None),
        check_vma=False,
    )
```

```python
import functools

import jax
import jax.numpy as jnp
from jax import lax
from jax.experimental import pallas as pl
from jax.experimental.pallas import tpu as pltpu
from jax.sharding import PartitionSpec as P

EPSILON = 1e-05
FAR = 64.0
F32 = jnp.float32
BF16 = jnp.bfloat16
ROWS = 144
LIMIT = 16 << 20
VMEM = pl.BlockSpec(memory_space=pltpu.VMEM)
FIXED = pl.BlockSpec(memory_space=pltpu.HBM)
SMEM = pl.BlockSpec(memory_space=pltpu.SMEM)


def iota(shape, dim):
    return lax.broadcasted_iota(jnp.int32, shape, dim)


def swap_lanes(x, step):
    if step == 64:
        return pltpu.roll(x, 64, 1)
    low = (iota(x.shape, 1) & step) == 0
    return jnp.where(low, pltpu.roll(x, 128 - step, 1), pltpu.roll(x, step, 1))


def pick_lanes(x, index):
    return jnp.take_along_axis(x, index, axis=1)


def split_row(row):
    index = 16 * iota((8, 128), 0) + (iota((8, 128), 1) & 15)
    return pick_lanes(jnp.broadcast_to(row, (8, 128)), index)


def split_rows(src, dst):
    lane = iota((8, 128), 1)
    for base in range(0, src.shape[0], 64):
        parts = [src[pl.ds(base + m, 8, stride=8), :] for m in range(8)]
        for bit in (4, 2, 1):
            step = 16 * bit
            low = (lane & step) == 0
            for m in range(8):
                if m & bit:
                    continue
                a, b = parts[m], parts[m + bit]
                parts[m] = jnp.where(low, a, pltpu.roll(b, step, 1))
                parts[m + bit] = jnp.where(low, pltpu.roll(a, 128 - step, 1), b)
        for q in range(8):
            dst[pl.ds(base + q, 8, stride=8), :] = parts[q]


def project_send(state, step, w_send, msg, flat, split):
    flat[...] = jnp.dot(state, w_send[step], preferred_element_type=F32)
    split_rows(flat, split)
    for cell in range(4):
        msg[cell, 0:128, :] = split[cell * 128 : cell * 128 + 128, :].astype(BF16)


def project_recv(state, step, w_recv, b_edge, w_disp, place, recv):
    r = jnp.dot(state, w_recv[step], preferred_element_type=F32) + b_edge[step : step + 1, :]
    r = r.astype(BF16).astype(F32)
    for cell in range(4):
        pull = sum(place[cell, k] * w_disp[k, step : step + 1, :] for k in range(3))
        recv[cell] = r[cell * 128 : cell * 128 + 128] - pull


def peers():
    me_len, me_wid = lax.axis_index("len"), lax.axis_index("wid")
    count = lax.axis_size("wid")
    right, left = lax.rem(me_wid + 1, count), lax.rem(me_wid + count - 1, count)
    return me_len, me_wid, left, right


def greet():
    me_len, me_wid, left, right = peers()
    other = 1 - me_len
    barrier = pltpu.get_barrier_semaphore()
    for peer in ((me_len, left), (me_len, right), (other, me_wid), (other, left), (other, right)):
        pl.semaphore_signal(barrier, inc=1, device_id=peer, device_id_type=pl.DeviceIdType.MESH)


def send_all(msg, grid, rows, send_sem, recv_sem, own_sem):
    me_len, me_wid, left, right = peers()
    other = 1 - me_len
    edge = 1 - me_len
    pl.semaphore_wait(pltpu.get_barrier_semaphore(), 5)
    plan = (
        (pl.ds(0, 2), pl.ds(6, 2), (me_len, left)),
        (pl.ds(2, 2), pl.ds(4, 2), (me_len, right)),
        (pl.ds(edge, 1), pl.ds(11, 1), (other, left)),
        (pl.ds(2 + edge, 1), pl.ds(8, 1), (other, right)),
        (pl.ds(edge, 1), pl.ds(9, 1), (other, me_wid)),
        (pl.ds(2 + edge, 1), pl.ds(10, 1), (other, me_wid)),
    )
    copies = []
    for k, (src, dst, peer) in enumerate(plan):
        copy = pltpu.make_async_remote_copy(
            src_ref=msg.at[src, pl.ds(0, rows)],
            dst_ref=grid.at[dst, pl.ds(0, rows)],
            send_sem=send_sem.at[k],
            recv_sem=recv_sem.at[k],
            device_id=peer,
            device_id_type=pl.DeviceIdType.MESH,
        )
        copy.start()
        copies.append(copy)
    own = pltpu.make_async_copy(msg.at[:, pl.ds(0, rows)], grid.at[pl.ds(0, 4), pl.ds(0, rows)], own_sem)
    own.start()
    return copies + [own]


def begin(latent_in, offset, occupied, w_send_in, w_recv_in, b_edge, w_disp, w_dist, codes, *refs):
    state, ranks, recv, place, grid, table, push_out, msg, flat, split, send_sem, recv_sem, own_sem = refs[:13]
    latent, w_send, w_recv, load_sem = refs[13:]
    greet()
    loads = [
        pltpu.make_async_copy(src, dst, load_sem.at[k])
        for k, (src, dst) in enumerate(((latent_in, latent), (w_send_in, w_send), (w_recv_in, w_recv)))
    ]
    for load in loads:
        load.start()
    occ = occupied[...].astype(F32)
    total = jnp.sum(occ, axis=1, keepdims=True)
    line, lane = iota((128, 128), 0), iota((128, 128), 1)
    slot = line.astype(F32)
    same = (line == lane).astype(F32).astype(BF16)
    both = (((1,), (1,)), ((), ()))
    perms = [None] * 4
    for row in range(2):
        for col in range(2):
            given, cell = row * 2 + col, col * 2 + row
            held = occ[given : given + 1]
            key = (offset[row, 1, col : col + 1, :].astype(F32) + 2.0 * (1.0 - held)).astype(BF16)
            key_row = jnp.broadcast_to(key.astype(F32), (128, 128))
            key_col = lax.dot_general(same, key_row.astype(BF16), both, preferred_element_type=F32)
            ahead = (key_col < key_row) | ((key_col == key_row) & (line < lane))
            rank = jnp.sum(ahead.astype(F32), axis=0, keepdims=True)
            ranks[given : given + 1, :] = rank
            perm = (slot == rank).astype(F32).astype(BF16)
            perms[cell] = perm
            geo = [offset[row, k, col : col + 1, :].astype(F32) for k in range(3)]
            geo = jnp.concatenate(geo + [held, jnp.zeros((12, 128), F32)], axis=0).astype(BF16)
            moved = lax.dot_general(geo, perm, both, preferred_element_type=F32)
            msg[cell, 128:ROWS, :] = moved.astype(BF16)
    for load in loads:
        load.wait()
    for cell in range(4):
        given = (cell & 1) * 2 + (cell >> 1)
        state[cell] = jnp.dot(perms[cell], latent[given], preferred_element_type=F32).astype(BF16)
    project_send(state[...].reshape(512, 128), 0, w_send, msg, flat, split)
    copies = send_all(msg, grid, ROWS, send_sem, recv_sem, own_sem)
    for row in range(2):
        for col in range(2):
            given, cell = row * 2 + col, col * 2 + row
            full = slot < total[given : given + 1, :]
            for k in range(3):
                part = jnp.broadcast_to(offset[row, k, col : col + 1, :].astype(F32), (128, 128)).astype(BF16)
                spread = lax.dot_general(perms[cell], part, both, preferred_element_type=F32)
                place[cell, k] = jnp.where(full, spread, -FAR) if k == 2 else spread
            parts = [place[cell, k] for k in range(3)]
            place[cell, 3] = 1.0 - parts[0] * parts[0] - parts[1] * parts[1] - parts[2] * parts[2]
    project_recv(state[...].reshape(512, 128), 0, w_recv, b_edge, w_disp, place, recv)
    for step in range(2):
        for k in range(3):
            line_of = 4 * step + k
            push_out[line_of : line_of + 1, :] = w_disp[k, step : step + 1, :]
        push_out[4 * step + 3 : 4 * step + 4, :] = w_dist[step : step + 1, :]
    wide_lane = iota((1, 128), 1)
    step = (wide_lane * 8) & 127
    tall = iota((16, 128), 0)
    table_lane = iota((64, 128), 1)
    tops, bottoms = [], []
    for cell in range(4):
        given = (cell & 1) * 2 + (cell >> 1)
        inside = (tall * 8 + 7).astype(F32) < total[given : given + 1, :]
        tops.append(jnp.where(inside, place[cell, 1, pl.ds(7, 16, stride=8), :], 2.0))
        bottoms.append(place[cell, 1, pl.ds(0, 16, stride=8), :])
    top, bottom = jnp.concatenate(tops, axis=0), jnp.concatenate(bottoms, axis=0)
    high, low = jnp.zeros((64, 128), F32), jnp.zeros((64, 128), F32)
    held = jnp.zeros((1, 128), F32)
    for copy in copies:
        copy.wait()
    for cell in range(12):
        geo = grid[cell, 128:ROWS, :].astype(F32)
        count = jnp.sum(geo[3:4], axis=1, keepdims=True)
        mine = table_lane == cell
        held = jnp.where(wide_lane == cell, count, held)
        at = (wide_lane * 8).astype(F32)
        begins = pick_lanes(jnp.broadcast_to(geo[1:2], (8, 128)), jnp.broadcast_to(step, (8, 128)))[0:1]
        ends = pick_lanes(jnp.broadcast_to(geo[1:2], (8, 128)), jnp.broadcast_to(step + 7, (8, 128)))[0:1]
        begins = jnp.where(at < count, begins, 4.0)
        ends = jnp.where(at + 7.0 < count, ends, 4.0)
        high = jnp.where(mine, jnp.sum((begins < top).astype(F32), axis=1, keepdims=True), high)
        low = jnp.where(mine, jnp.sum((ends <= bottom).astype(F32), axis=1, keepdims=True), low)
    table[0:64, :] = high.astype(jnp.int32)
    table[64:128, :] = low.astype(jnp.int32)
    table[128:136, :] = jnp.broadcast_to(held, (8, 128)).astype(jnp.int32)
    table[129:130, 0 : codes.shape[1]] = codes[...]


def node_update(step, state, msg_in, w_self, w_msg, b_node, w_out, gain):
    h = state[...].reshape(512, 128)
    pre = (
        jnp.dot(h, w_self[step], preferred_element_type=F32)
        + jnp.dot(msg_in, w_msg[step], preferred_element_type=F32)
        + b_node[step : step + 1, :]
    )
    hidden = jnp.maximum(pre, 0.0).astype(BF16)
    y = jnp.dot(hidden, w_out[step], preferred_element_type=F32)
    center = jnp.mean(y, axis=-1, keepdims=True)
    spread = jnp.mean(jnp.square(y - center), axis=-1, keepdims=True)
    normed = (y - center) / jnp.sqrt(spread + EPSILON)
    return (h.astype(F32) + normed * gain[step : step + 1, :]).astype(BF16)


def middle(state, msg_in, before, place, w_send, w_recv, b_edge, w_disp, *refs):
    w_self, w_msg, b_node, w_out, gain = refs[:5]
    state_out, recv, grid, msg, flat, split, send_sem, recv_sem, own_sem = refs[5:]
    greet()
    new = node_update(0, state, msg_in[...], w_self, w_msg, b_node, w_out, gain)
    state_out[...] = new.reshape(4, 128, 128)
    project_send(new, 1, w_send, msg, flat, split)
    copies = send_all(msg, grid, 128, send_sem, recv_sem, own_sem)
    project_recv(new, 1, w_recv, b_edge, w_disp, place, recv)
    for cell in range(12):
        grid[cell, 128:ROWS, :] = before[cell, 128:ROWS, :]
    for copy in copies:
        copy.wait()


def pairs(step, last, table, grid, recv, place, weights, *refs):
    if last:
        state, ranks, w_self, w_msg, b_node, w_out, gain, out = refs[:8]
        rest = refs[8:]
    else:
        (msg_in,) = refs[:1]
        rest = refs[1:]
    acc, floor, csum, sent, queue, spots, feats, far, close, incoming, plan, many = rest
    me_len = lax.axis_index("len")
    counts = [table[128, cell] for cell in range(4)]

    for cell in range(12):
        geo = grid[cell, 128:ROWS, :].astype(F32)
        for k in range(3):
            row = geo[k : k + 1]
            if k == 2:
                row = row + FAR * (1.0 - geo[3:4])
            row = jnp.broadcast_to(row, (8, 128))
            index = 8 * iota((8, 128), 0) + (iota((8, 128), 1) >> 4)
            spots[cell, k, 0:8, :] = pick_lanes(row, index)
            spots[cell, k, 8:16, :] = pick_lanes(row, index + 64)
            spots[cell, k, 16:24, :] = jnp.full((8, 128), FAR)

    acc[...] = jnp.zeros_like(acc)
    csum[...] = jnp.zeros_like(csum)
    incoming[...] = jnp.zeros_like(incoming)

    for cell in range(4):

        def spread_recv(group, _, cell=cell):
            for t in range(4):
                at = pl.multiple_of(group * 32 + 8 * t, 8)
                x = -recv[cell, pl.ds(at, 8), :]
                for q in range(8):
                    part = pick_lanes(x, 16 * q + (iota((8, 128), 1) & 15))
                    floor[pl.ds((cell * 128 + at) * 8 + q, 8, stride=8), :] = part
            return 0

        lax.fori_loop(0, (counts[cell] + 31) >> 5, spread_recv, 0)

    push = [split_row(weights[4 * step + k : 4 * step + k + 1, :]) for k in range(3)]
    pull = split_row(weights[4 * step + 3 : 4 * step + 4, :])

    for cell in range(4):
        many[cell] = 0

    def enlist(p, _):
        code = table[129, p]
        given = (code * 57) >> 9
        direction = code - given * 9
        row, col = given >> 1, given & 1
        high = (direction * 11) >> 5
        up, side = high - 1, direction - high * 3 - 1
        cell = col * 2 + row
        at_row, at_col = row + 1 + up, col + 1 + side
        in_rows = (at_row == 1) | (at_row == 2)
        in_cols = (at_col == 1) | (at_col == 2)
        beyond = at_row == jnp.where(me_len == 0, 3, 0)
        source = jnp.where(
            in_rows & in_cols,
            (at_col - 1) * 2 + at_row - 1,
            jnp.where(in_rows, jnp.where(at_col == 3, 6, 4) + at_row - 1, 8 + at_col),
        )

        @pl.when(in_rows | beyond)
        def _():
            spot = many[cell]
            plan[cell, 3 * spot] = source
            plan[cell, 3 * spot + 1] = up
            plan[cell, 3 * spot + 2] = side
            many[cell] = spot + 1

        return 0

    listed = sum((table[129, p] >= 0).astype(jnp.int32) for p in range(36))
    lax.fori_loop(0, listed, enlist, 0)

    def one_cell(cell, _):
        here, entries = table[128, cell], many[cell]

        def fill(q, _):
            source, up, side = (plan[cell, 3 * q + k] for k in range(3))
            shift = [jnp.full((1, 128), s.astype(F32)) for s in (up, side)]

            x, y, z = spots[source, 0] + shift[0], spots[source, 1] + shift[1], spots[source, 2]
            feats[q, 0], feats[q, 1], feats[q, 2] = x + x, y + y, z + z
            feats[q, 3] = -(x * x + y * y + z * z)

            def some(b, _):
                for r in range(4):
                    at = b * 4 + r
                    ox, oy, oz = (feats[q, k, pl.ds(at, 1), :] * 0.5 for k in range(3))
                    s = grid[source, pl.ds(pl.multiple_of(at * 8, 8), 8), :].astype(F32)
                    put = pl.ds(pl.multiple_of(q * 160 + at * 8, 8), 8)
                    sent[put, :] = (s + ox * push[0] + oy * push[1] + oz * push[2]) + pull
                return 0

            return lax.fori_loop(0, (table[128, source] + 31) >> 5, some, 0)

        lax.fori_loop(0, entries, fill, 0)

        def block_of(tiles, tile):
            size = 8 * tiles
            start = pl.multiple_of(cell * 128 + tile * 8, 8)
            rows = [pl.ds(pl.multiple_of(tile * 8 + 8 * t, 8), 8) for t in range(tiles)]
            own = [[place[cell, k, rows[t], :] for k in range(4)] for t in range(tiles)]

            def measure(q, carry):
                front, weight = carry[0], carry[1:]
                source, side = plan[cell, 3 * q], plan[cell, 3 * q + 2]
                lines = (table[128, source] + 7) >> 3
                most = jnp.where(side == 1, table[cell * 16 + tile + tiles - 1, source], lines)
                least = jnp.where(side == -1, table[64 + cell * 16 + tile, source], 0)
                span = jnp.maximum(most - least, 0)

                def some(b, weight):
                    weight = list(weight)
                    for r in range(4):
                        at, to = least + b * 4 + r, front + b * 4 + r
                        x, y, z, base = (feats[q, k, pl.ds(at, 1), :] for k in range(4))
                        take = pl.ds(pl.multiple_of(q * 160 + at * 8, 8), 8)
                        queue[pl.ds(pl.multiple_of(to * 8, 8), 8), :] = sent[take, :]
                        for t in range(tiles):
                            ox, oy, oz, mine = own[t]
                            d = (mine + base) + ox * x + oy * y + oz * z
                            c = jnp.maximum(d, 0.0)
                            c = c * c
                            put = pl.ds(pl.multiple_of(to * 16 + 8 * t, 8), 8)
                            far[put, :] = d
                            close[put, :] = c
                            weight[t] = weight[t] + c
                    return tuple(weight)

                weight = lax.fori_loop(0, (span + 3) >> 2, some, weight)
                return (front + span,) + tuple(weight)

            nothing = jnp.zeros((8, 128), F32)
            carry = lax.fori_loop(0, entries, measure, (jnp.int32(0),) + (nothing,) * tiles)
            front = carry[0]
            for t in range(tiles):
                csum[pl.ds(start + 8 * t, 8), :] = carry[1 + t]
            for r in range(3):
                queue[pl.ds(pl.multiple_of((front + r) * 8, 8), 8), :] = nothing
                for t in range(tiles):
                    far[pl.ds(pl.multiple_of((front + r) * 16 + 8 * t, 8), 8), :] = nothing
                    close[pl.ds(pl.multiple_of((front + r) * 16 + 8 * t, 8), 8), :] = nothing

            first = pl.multiple_of(start * 8, 64)
            nr = [floor[pl.ds(first + 8 * i, 8), :] for i in range(size)]

            def senders(b, carry):
                sums = list(carry)
                for r in range(4):
                    at = b * 4 + r
                    s = queue[pl.ds(pl.multiple_of(at * 8, 8), 8), :]
                    for i in range(size):
                        d = far[pl.ds(at * 16 + i, 1), :]
                        c = close[pl.ds(at * 16 + i, 1), :]
                        sums[i] = sums[i] + c * jnp.maximum(s - d * pull, nr[i])
                return tuple(sums)

            sums = lax.fori_loop(0, (front + 3) >> 2, senders, (nothing,) * size)
            for i in range(size):
                acc[pl.ds(first + 8 * i, 8), :] = sums[i]

        def pair_of_tiles(b, _):
            block_of(2, 2 * b)
            return 0

        def odd_tile(b, _):
            block_of(1, b)
            return 0

        tiles = (here + 7) >> 3
        lax.fori_loop(0, tiles >> 1, pair_of_tiles, 0)
        lax.fori_loop(tiles & ~1, tiles, odd_tile, 0)
        return 0

    lax.fori_loop(0, 4, one_cell, 0)

    for cell in range(4):

        def gather(group, _, cell=cell):
            lane = iota((8, 128), 1)
            for t in range(4):
                at = pl.multiple_of(group * 32 + 8 * t, 8)
                base = (cell * 128 + at) * 8
                parts = [acc[pl.ds(base + q, 8, stride=8), :] for q in range(8)]
                for bit in (4, 2, 1):
                    low = (lane & (16 * bit)) == 0
                    parts = [
                        jnp.where(low, parts[q], parts[q + bit])
                        + swap_lanes(jnp.where(low, parts[q + bit], parts[q]), 16 * bit)
                        for q in range(bit)
                    ]
                weight = jnp.sum(csum[pl.ds(cell * 128 + at, 8), :], axis=1, keepdims=True) * (1.0 / 16.0)
                incoming[pl.ds(cell * 128 + at, 8), :] = parts[0] + recv[cell, pl.ds(at, 8), :] * weight
            return 0

        lax.fori_loop(0, (counts[cell] + 31) >> 5, gather, 0)

    rounded = (incoming[...] * (8.0 / 128.0)).astype(BF16)
    if not last:
        msg_in[...] = rounded
        return
    new = node_update(step, state, rounded, w_self, w_msg, b_node, w_out, gain)
    slot = iota((128, 128), 0).astype(F32)
    for cell in range(4):
        given = (cell & 1) * 2 + (cell >> 1)
        perm = (slot == ranks[given : given + 1, :]).astype(F32).astype(BF16)
        here = new[cell * 128 : cell * 128 + 128]
        back = lax.dot_general(perm, here, (((0,), (0,)), ((), ())), preferred_element_type=F32)
        out[given] = back.astype(BF16)


def per_device(
    latent, offset, occupied, pair_list, w_send, w_recv, b_edge, w_disp, w_dist, w_self, w_msg, b_node, w_out, gain
):
    shape = jax.ShapeDtypeStruct
    w_disp = w_disp.transpose(1, 0, 2)
    sems = [pltpu.SemaphoreType.DMA((6,)), pltpu.SemaphoreType.DMA((6,)), pltpu.SemaphoreType.DMA]
    work = [pltpu.VMEM((4, ROWS, 128), BF16), pltpu.VMEM((512, 128), F32), pltpu.VMEM((512, 128), F32)]
    cells, wide = shape((4, 128, 128), BF16), shape((4, 128, 128), F32)
    state, ranks, recv, place, grid, table, weights = pl.pallas_call(
        begin,
        name="begin",
        out_shape=(
            cells,
            shape((4, 128), F32),
            wide,
            shape((4, 4, 128, 128), F32),
            shape((12, ROWS, 128), BF16),
            shape((136, 128), jnp.int32),
            shape((8, 128), F32),
        ),
        in_specs=[FIXED, VMEM, VMEM, FIXED, FIXED] + [VMEM] * 4,
        out_specs=(VMEM,) * 7,
        scratch_shapes=work
        + sems
        + [pltpu.VMEM((4, 128, 128), BF16), pltpu.VMEM((2, 128, 128), BF16), pltpu.VMEM((2, 128, 128), BF16)]
        + [pltpu.SemaphoreType.DMA((3,))],
        compiler_params=pltpu.CompilerParams(collective_id=0, has_side_effects=True, vmem_limit_bytes=LIMIT),
    )(
        *(
            pltpu.with_memory_space_constraint(x, pltpu.HBM)
            for x in (
                latent.reshape(4, 128, 128),
                offset.transpose(0, 2, 1, 3),
                occupied.reshape(4, 128),
                w_send,
                w_recv,
                b_edge,
                w_disp,
                w_dist,
                pair_list.reshape(1, -1),
            )
        )
    )
    scratch = [
        pltpu.VMEM((4096, 128), F32),
        pltpu.VMEM((4096, 128), F32),
        pltpu.VMEM((512, 128), F32),
        pltpu.VMEM((9 * 160, 128), F32),
        pltpu.VMEM((148 * 8, 128), F32),
        pltpu.VMEM((12, 3, 24, 128), F32),
        pltpu.VMEM((9, 4, 24, 128), F32),
        pltpu.VMEM((148 * 16, 128), F32),
        pltpu.VMEM((148 * 16, 128), F32),
        pltpu.VMEM((512, 128), F32),
        pltpu.SMEM((4, 27), jnp.int32),
        pltpu.SMEM((4,), jnp.int32),
    ]
    msg_in = pl.pallas_call(
        functools.partial(pairs, 0, False),
        name="pairs_0",
        out_shape=shape((512, 128), BF16),
        in_specs=[SMEM] + [VMEM] * 4,
        out_specs=VMEM,
        scratch_shapes=scratch,
        compiler_params=pltpu.CompilerParams(vmem_limit_bytes=LIMIT),
    )(table, grid, recv, place, weights)
    state, recv, grid = pl.pallas_call(
        middle,
        name="middle",
        out_shape=(cells, wide, shape((12, ROWS, 128), BF16)),
        in_specs=[VMEM] * 13,
        out_specs=(VMEM,) * 3,
        scratch_shapes=work + sems,
        compiler_params=pltpu.CompilerParams(collective_id=1, has_side_effects=True, vmem_limit_bytes=LIMIT),
    )(state, msg_in, grid, place, w_send, w_recv, b_edge, w_disp, w_self, w_msg, b_node, w_out, gain)
    out = pl.pallas_call(
        functools.partial(pairs, 1, True),
        name="pairs_1",
        out_shape=cells,
        in_specs=[SMEM] + [VMEM] * 11,
        out_specs=VMEM,
        scratch_shapes=scratch,
        compiler_params=pltpu.CompilerParams(vmem_limit_bytes=LIMIT),
    )(table, grid, recv, place, weights, state, ranks, w_self, w_msg, b_node, w_out, gain)
    return out.reshape(latent.shape)


def solution(mesh):
    return jax.shard_map(
        per_device,
        mesh=mesh,
        in_specs=(
            P("len", "wid", None, None),
            P("len", "wid", None, None),
            P("len", "wid", None),
            P("len", "wid", None),
        )
        + (P(),) * 10,
        out_specs=P("len", "wid", None, None),
        check_vma=False,
    )
```

```python
import functools

import jax
import jax.numpy as jnp
from jax import lax
from jax.experimental import pallas as pl
from jax.experimental.pallas import tpu as pltpu
from jax.sharding import PartitionSpec as P

EPSILON = 1e-05
FAR = 64.0
F32 = jnp.float32
BF16 = jnp.bfloat16
ROWS = 144
LIMIT = 16 << 20
VMEM = pl.BlockSpec(memory_space=pltpu.VMEM)
FIXED = pl.BlockSpec(memory_space=pltpu.HBM)
SMEM = pl.BlockSpec(memory_space=pltpu.SMEM)


def iota(shape, dim):
    return lax.broadcasted_iota(jnp.int32, shape, dim)


def swap_lanes(x, step):
    if step == 64:
        return pltpu.roll(x, 64, 1)
    low = (iota(x.shape, 1) & step) == 0
    return jnp.where(low, pltpu.roll(x, 128 - step, 1), pltpu.roll(x, step, 1))


def pick_lanes(x, index):
    return jnp.take_along_axis(x, index, axis=1)


def split_row(row):
    index = 16 * iota((8, 128), 0) + (iota((8, 128), 1) & 15)
    return pick_lanes(jnp.broadcast_to(row, (8, 128)), index)


def split_rows(src, dst):
    lane = iota((8, 128), 1)
    for base in range(0, src.shape[0], 64):
        parts = [src[pl.ds(base + m, 8, stride=8), :] for m in range(8)]
        for bit in (4, 2, 1):
            step = 16 * bit
            low = (lane & step) == 0
            for m in range(8):
                if m & bit:
                    continue
                a, b = parts[m], parts[m + bit]
                parts[m] = jnp.where(low, a, pltpu.roll(b, step, 1))
                parts[m + bit] = jnp.where(low, pltpu.roll(a, 128 - step, 1), b)
        for q in range(8):
            dst[pl.ds(base + q, 8, stride=8), :] = parts[q]


def project_send(state, step, w_send, msg, flat, split):
    flat[...] = jnp.dot(state, w_send[step], preferred_element_type=F32)
    split_rows(flat, split)
    for cell in range(4):
        msg[cell, 0:128, :] = split[cell * 128 : cell * 128 + 128, :].astype(BF16)


def project_recv(state, step, w_recv, b_edge, w_disp, place, recv):
    r = jnp.dot(state, w_recv[step], preferred_element_type=F32) + b_edge[step : step + 1, :]
    r = r.astype(BF16).astype(F32)
    for cell in range(4):
        pull = sum(place[cell, k] * w_disp[k, step : step + 1, :] for k in range(3))
        recv[cell] = r[cell * 128 : cell * 128 + 128] - pull


def spread_recv(recv, floor):
    def some(group, _):
        for t in range(4):
            tile = group * 4 + t
            x = -recv[tile >> 4, pl.ds(pl.multiple_of((tile & 15) * 8, 8), 8), :]
            for q in range(8):
                floor[pl.ds(tile * 64 + q, 8, stride=8), :] = pick_lanes(x, 16 * q + (iota((8, 128), 1) & 15))
        return 0

    lax.fori_loop(0, 16, some, 0)


def peers():
    me_len, me_wid = lax.axis_index("len"), lax.axis_index("wid")
    count = lax.axis_size("wid")
    right, left = lax.rem(me_wid + 1, count), lax.rem(me_wid + count - 1, count)
    return me_len, me_wid, left, right


def greet():
    me_len, me_wid, left, right = peers()
    other = 1 - me_len
    barrier = pltpu.get_barrier_semaphore()
    for peer in ((me_len, left), (me_len, right), (other, me_wid), (other, left), (other, right)):
        pl.semaphore_signal(barrier, inc=1, device_id=peer, device_id_type=pl.DeviceIdType.MESH)


def send_all(msg, grid, rows, send_sem, recv_sem, own_sem):
    me_len, me_wid, left, right = peers()
    other = 1 - me_len
    edge = 1 - me_len
    pl.semaphore_wait(pltpu.get_barrier_semaphore(), 5)
    plan = (
        (pl.ds(0, 2), pl.ds(6, 2), (me_len, left)),
        (pl.ds(2, 2), pl.ds(4, 2), (me_len, right)),
        (pl.ds(edge, 1), pl.ds(11, 1), (other, left)),
        (pl.ds(2 + edge, 1), pl.ds(8, 1), (other, right)),
        (pl.ds(edge, 1), pl.ds(9, 1), (other, me_wid)),
        (pl.ds(2 + edge, 1), pl.ds(10, 1), (other, me_wid)),
    )
    copies = []
    for k, (src, dst, peer) in enumerate(plan):
        copy = pltpu.make_async_remote_copy(
            src_ref=msg.at[src, pl.ds(0, rows)],
            dst_ref=grid.at[dst, pl.ds(0, rows)],
            send_sem=send_sem.at[k],
            recv_sem=recv_sem.at[k],
            device_id=peer,
            device_id_type=pl.DeviceIdType.MESH,
        )
        copy.start()
        copies.append(copy)
    own = pltpu.make_async_copy(msg.at[:, pl.ds(0, rows)], grid.at[pl.ds(0, 4), pl.ds(0, rows)], own_sem)
    own.start()
    return copies + [own]


def begin(latent_in, offset, occupied, w_send_in, w_recv_in, b_edge, w_disp, w_dist, codes, *refs):
    state, ranks, recv, place, grid, table, push_out, floor, spots = refs[:9]
    msg, flat, split, send_sem, recv_sem, own_sem, latent, w_send, w_recv, load_sem = refs[9:]
    greet()
    loads = [
        pltpu.make_async_copy(src, dst, load_sem.at[k])
        for k, (src, dst) in enumerate(((latent_in, latent), (w_send_in, w_send), (w_recv_in, w_recv)))
    ]
    for load in loads:
        load.start()
    occ = occupied[...].astype(F32)
    total = jnp.sum(occ, axis=1, keepdims=True)
    line, lane = iota((128, 128), 0), iota((128, 128), 1)
    slot = line.astype(F32)
    same = (line == lane).astype(F32).astype(BF16)
    both = (((1,), (1,)), ((), ()))
    perms = [None] * 4
    for row in range(2):
        for col in range(2):
            given, cell = row * 2 + col, col * 2 + row
            held = occ[given : given + 1]
            key = (offset[row, 1, col : col + 1, :].astype(F32) + 2.0 * (1.0 - held)).astype(BF16)
            key_row = jnp.broadcast_to(key.astype(F32), (128, 128))
            key_col = lax.dot_general(same, key_row.astype(BF16), both, preferred_element_type=F32)
            ahead = (key_col < key_row) | ((key_col == key_row) & (line < lane))
            rank = jnp.sum(ahead.astype(F32), axis=0, keepdims=True)
            ranks[given : given + 1, :] = rank
            perm = (slot == rank).astype(F32).astype(BF16)
            perms[cell] = perm
            geo = [offset[row, k, col : col + 1, :].astype(F32) for k in range(3)]
            geo = jnp.concatenate(geo + [held, jnp.zeros((12, 128), F32)], axis=0).astype(BF16)
            moved = lax.dot_general(geo, perm, both, preferred_element_type=F32)
            msg[cell, 128:ROWS, :] = moved.astype(BF16)
    for load in loads:
        load.wait()
    for cell in range(4):
        given = (cell & 1) * 2 + (cell >> 1)
        state[cell] = jnp.dot(perms[cell], latent[given], preferred_element_type=F32).astype(BF16)
    project_send(state[...].reshape(512, 128), 0, w_send, msg, flat, split)
    copies = send_all(msg, grid, ROWS, send_sem, recv_sem, own_sem)
    for row in range(2):
        for col in range(2):
            given, cell = row * 2 + col, col * 2 + row
            full = slot < total[given : given + 1, :]
            for k in range(3):
                part = jnp.broadcast_to(offset[row, k, col : col + 1, :].astype(F32), (128, 128)).astype(BF16)
                spread = lax.dot_general(perms[cell], part, both, preferred_element_type=F32)
                place[cell, k] = jnp.where(full, spread, -FAR) if k == 2 else spread
            parts = [place[cell, k] for k in range(3)]
            place[cell, 3] = 1.0 - parts[0] * parts[0] - parts[1] * parts[1] - parts[2] * parts[2]
    project_recv(state[...].reshape(512, 128), 0, w_recv, b_edge, w_disp, place, recv)
    spread_recv(recv, floor)
    for step in range(2):
        for k in range(3):
            line_of = 4 * step + k
            push_out[line_of : line_of + 1, :] = w_disp[k, step : step + 1, :]
        push_out[4 * step + 3 : 4 * step + 4, :] = w_dist[step : step + 1, :]
    wide_lane = iota((1, 128), 1)
    step = (wide_lane * 8) & 127
    tall = iota((16, 128), 0)
    table_lane = iota((64, 128), 1)
    tops, bottoms = [], []
    for cell in range(4):
        given = (cell & 1) * 2 + (cell >> 1)
        inside = (tall * 8 + 7).astype(F32) < total[given : given + 1, :]
        tops.append(jnp.where(inside, place[cell, 1, pl.ds(7, 16, stride=8), :], 2.0))
        bottoms.append(place[cell, 1, pl.ds(0, 16, stride=8), :])
    top, bottom = jnp.concatenate(tops, axis=0), jnp.concatenate(bottoms, axis=0)
    high, low = jnp.zeros((64, 128), F32), jnp.zeros((64, 128), F32)
    held = jnp.zeros((1, 128), F32)
    for copy in copies:
        copy.wait()
    for cell in range(12):
        geo = grid[cell, 128:ROWS, :].astype(F32)
        count = jnp.sum(geo[3:4], axis=1, keepdims=True)
        mine = table_lane == cell
        held = jnp.where(wide_lane == cell, count, held)
        at = (wide_lane * 8).astype(F32)
        begins = pick_lanes(jnp.broadcast_to(geo[1:2], (8, 128)), jnp.broadcast_to(step, (8, 128)))[0:1]
        ends = pick_lanes(jnp.broadcast_to(geo[1:2], (8, 128)), jnp.broadcast_to(step + 7, (8, 128)))[0:1]
        begins = jnp.where(at < count, begins, 4.0)
        ends = jnp.where(at + 7.0 < count, ends, 4.0)
        high = jnp.where(mine, jnp.sum((begins < top).astype(F32), axis=1, keepdims=True), high)
        low = jnp.where(mine, jnp.sum((ends <= bottom).astype(F32), axis=1, keepdims=True), low)
    both_sides = jnp.concatenate([high, low], axis=0).T
    table[0:16, :] = both_sides[0:16].astype(jnp.int32)
    table[16:24, :] = jnp.broadcast_to(held, (8, 128)).astype(jnp.int32)
    table[17:18, 0 : codes.shape[1]] = codes[...]

    for cell in range(12):
        geo = grid[cell, 128:ROWS, :].astype(F32)
        for k in range(3):
            row = geo[k : k + 1]
            if k == 2:
                row = row + FAR * (1.0 - geo[3:4])
            row = jnp.broadcast_to(row, (8, 128))
            index = 8 * iota((8, 128), 0) + (iota((8, 128), 1) >> 4)
            spots[cell, k, 0:8, :] = pick_lanes(row, index)
            spots[cell, k, 8:16, :] = pick_lanes(row, index + 64)
            spots[cell, k, 16:24, :] = jnp.full((8, 128), FAR)


def node_update(step, state, msg_in, w_self, w_msg, b_node, w_out, gain):
    h = state[...].reshape(512, 128)
    pre = (
        jnp.dot(h, w_self[step], preferred_element_type=F32)
        + jnp.dot(msg_in, w_msg[step], preferred_element_type=F32)
        + b_node[step : step + 1, :]
    )
    hidden = jnp.maximum(pre, 0.0).astype(BF16)
    y = jnp.dot(hidden, w_out[step], preferred_element_type=F32)
    center = jnp.mean(y, axis=-1, keepdims=True)
    spread = jnp.mean(jnp.square(y - center), axis=-1, keepdims=True)
    normed = (y - center) / jnp.sqrt(spread + EPSILON)
    return (h.astype(F32) + normed * gain[step : step + 1, :]).astype(BF16)


def middle(state, msg_in, before, place, w_send, w_recv, b_edge, w_disp, *refs):
    w_self, w_msg, b_node, w_out, gain = refs[:5]
    state_out, recv, grid, floor, msg, flat, split, send_sem, recv_sem, own_sem = refs[5:]
    greet()
    new = node_update(0, state, msg_in[...], w_self, w_msg, b_node, w_out, gain)
    state_out[...] = new.reshape(4, 128, 128)
    project_send(new, 1, w_send, msg, flat, split)
    copies = send_all(msg, grid, 128, send_sem, recv_sem, own_sem)
    project_recv(new, 1, w_recv, b_edge, w_disp, place, recv)
    spread_recv(recv, floor)
    for cell in range(12):
        grid[cell, 128:ROWS, :] = before[cell, 128:ROWS, :]
    for copy in copies:
        copy.wait()


def pairs(step, last, table, grid, recv, place, weights, spots, floor, *refs):
    if last:
        state, ranks, w_self, w_msg, b_node, w_out, gain, out = refs[:8]
        rest = refs[8:]
    else:
        (msg_in,) = refs[:1]
        rest = refs[1:]
    acc, csum, sent, queue, feats, far, close, incoming, plan, many = rest
    me_len = lax.axis_index("len")
    counts = [table[16, cell] for cell in range(4)]

    acc[...] = jnp.zeros_like(acc)
    csum[...] = jnp.zeros_like(csum)
    incoming[...] = jnp.zeros_like(incoming)

    push = [split_row(weights[4 * step + k : 4 * step + k + 1, :]) for k in range(3)]
    pull = split_row(weights[4 * step + 3 : 4 * step + 4, :])

    for cell in range(4):
        many[cell] = 0

    def enlist(p, _):
        code = table[17, p]
        given = (code * 57) >> 9
        direction = code - given * 9
        row, col = given >> 1, given & 1
        high = (direction * 11) >> 5
        up, side = high - 1, direction - high * 3 - 1
        cell = col * 2 + row
        at_row, at_col = row + 1 + up, col + 1 + side
        in_rows = (at_row == 1) | (at_row == 2)
        in_cols = (at_col == 1) | (at_col == 2)
        beyond = at_row == jnp.where(me_len == 0, 3, 0)
        source = jnp.where(
            in_rows & in_cols,
            (at_col - 1) * 2 + at_row - 1,
            jnp.where(in_rows, jnp.where(at_col == 3, 6, 4) + at_row - 1, 8 + at_col),
        )

        @pl.when(in_rows | beyond)
        def _():
            spot = many[cell]
            plan[cell, 3 * spot] = source
            plan[cell, 3 * spot + 1] = up
            plan[cell, 3 * spot + 2] = side
            many[cell] = spot + 1

        return 0

    listed = sum((table[17, p] >= 0).astype(jnp.int32) for p in range(36))
    lax.fori_loop(0, listed, enlist, 0)

    def one_cell(cell, _):
        here, entries = table[16, cell], many[cell]

        def fill(q, _):
            source, up, side = (plan[cell, 3 * q + k] for k in range(3))
            shift = [jnp.full((1, 128), s.astype(F32)) for s in (up, side)]

            x, y, z = spots[source, 0] + shift[0], spots[source, 1] + shift[1], spots[source, 2]
            feats[q, 0], feats[q, 1], feats[q, 2] = x + x, y + y, z + z
            feats[q, 3] = -(x * x + y * y + z * z)

            for at in range(16):
                r = slice(at, at + 1)
                t = grid[source, at * 8 : at * 8 + 8, :].astype(F32) + pull
                sent[pl.ds(pl.multiple_of(q * 160 + at * 8, 8), 8), :] = (
                    t + x[r] * push[0] + y[r] * push[1] + z[r] * push[2]
                )
            return 0

        lax.fori_loop(0, entries, fill, 0)

        def block_of(tiles, tile):
            size = 8 * tiles
            start = pl.multiple_of(cell * 128 + tile * 8, 8)
            rows = [pl.ds(pl.multiple_of(tile * 8 + 8 * t, 8), 8) for t in range(tiles)]
            own = [[place[cell, k, rows[t], :] for k in range(4)] for t in range(tiles)]

            def measure(q, carry):
                front, weight = carry[0], carry[1:]
                source, side = plan[cell, 3 * q], plan[cell, 3 * q + 2]
                lines = (table[16, source] + 7) >> 3
                most = jnp.where(side == 1, table[source, cell * 16 + tile + tiles - 1], lines)
                least = jnp.where(side == -1, table[source, 64 + cell * 16 + tile], 0)
                span = jnp.maximum(most - least, 0)

                def some(b, weight):
                    weight = list(weight)
                    for r in range(4):
                        at, to = least + b * 4 + r, front + b * 4 + r
                        x, y, z, base = (feats[q, k, pl.ds(at, 1), :] for k in range(4))
                        take = pl.ds(pl.multiple_of(q * 160 + at * 8, 8), 8)
                        queue[pl.ds(pl.multiple_of(to * 8, 8), 8), :] = sent[take, :]
                        for t in range(tiles):
                            ox, oy, oz, mine = own[t]
                            d = (mine + base) + ox * x + oy * y + oz * z
                            c = jnp.maximum(d, 0.0)
                            c = c * c
                            put = pl.ds(pl.multiple_of(to * 16 + 8 * t, 8), 8)
                            far[put, :] = d
                            close[put, :] = c
                            weight[t] = weight[t] + c
                    return tuple(weight)

                weight = lax.fori_loop(0, (span + 3) >> 2, some, weight)
                return (front + span,) + tuple(weight)

            nothing = jnp.zeros((8, 128), F32)
            carry = lax.fori_loop(0, entries, measure, (jnp.int32(0),) + (nothing,) * tiles)
            front = carry[0]
            for t in range(tiles):
                csum[pl.ds(start + 8 * t, 8), :] = carry[1 + t]
            for r in range(3):
                queue[pl.ds(pl.multiple_of((front + r) * 8, 8), 8), :] = nothing
                for t in range(tiles):
                    far[pl.ds(pl.multiple_of((front + r) * 16 + 8 * t, 8), 8), :] = nothing
                    close[pl.ds(pl.multiple_of((front + r) * 16 + 8 * t, 8), 8), :] = nothing

            first = pl.multiple_of(start * 8, 64)
            nr = [floor[pl.ds(first + 8 * i, 8), :] for i in range(size)]

            def senders(b, carry):
                sums = list(carry)
                for r in range(4):
                    at = b * 4 + r
                    s = queue[pl.ds(pl.multiple_of(at * 8, 8), 8), :]
                    for i in range(size):
                        d = far[pl.ds(at * 16 + i, 1), :]
                        c = close[pl.ds(at * 16 + i, 1), :]
                        sums[i] = sums[i] + c * jnp.maximum(s - d * pull, nr[i])
                return tuple(sums)

            sums = lax.fori_loop(0, (front + 3) >> 2, senders, (nothing,) * size)
            for i in range(size):
                acc[pl.ds(first + 8 * i, 8), :] = sums[i]

        def pair_of_tiles(b, _):
            block_of(2, 2 * b)
            return 0

        def odd_tile(b, _):
            block_of(1, b)
            return 0

        tiles = (here + 7) >> 3
        lax.fori_loop(0, tiles >> 1, pair_of_tiles, 0)
        lax.fori_loop(tiles & ~1, tiles, odd_tile, 0)
        return 0

    lax.fori_loop(0, 4, one_cell, 0)

    for cell in range(4):

        def gather(group, _, cell=cell):
            lane = iota((8, 128), 1)
            for t in range(4):
                at = pl.multiple_of(group * 32 + 8 * t, 8)
                base = (cell * 128 + at) * 8
                parts = [acc[pl.ds(base + q, 8, stride=8), :] for q in range(8)]
                for bit in (4, 2, 1):
                    low = (lane & (16 * bit)) == 0
                    parts = [
                        jnp.where(low, parts[q], parts[q + bit])
                        + swap_lanes(jnp.where(low, parts[q + bit], parts[q]), 16 * bit)
                        for q in range(bit)
                    ]
                weight = jnp.sum(csum[pl.ds(cell * 128 + at, 8), :], axis=1, keepdims=True) * (1.0 / 16.0)
                incoming[pl.ds(cell * 128 + at, 8), :] = parts[0] + recv[cell, pl.ds(at, 8), :] * weight
            return 0

        lax.fori_loop(0, (counts[cell] + 31) >> 5, gather, 0)

    rounded = (incoming[...] * (8.0 / 128.0)).astype(BF16)
    if not last:
        msg_in[...] = rounded
        return
    new = node_update(step, state, rounded, w_self, w_msg, b_node, w_out, gain)
    slot = iota((128, 128), 0).astype(F32)
    for cell in range(4):
        given = (cell & 1) * 2 + (cell >> 1)
        perm = (slot == ranks[given : given + 1, :]).astype(F32).astype(BF16)
        here = new[cell * 128 : cell * 128 + 128]
        back = lax.dot_general(perm, here, (((0,), (0,)), ((), ())), preferred_element_type=F32)
        out[given] = back.astype(BF16)


def per_device(
    latent, offset, occupied, pair_list, w_send, w_recv, b_edge, w_disp, w_dist, w_self, w_msg, b_node, w_out, gain
):
    shape = jax.ShapeDtypeStruct
    w_disp = w_disp.transpose(1, 0, 2)
    sems = [pltpu.SemaphoreType.DMA((6,)), pltpu.SemaphoreType.DMA((6,)), pltpu.SemaphoreType.DMA]
    work = [pltpu.VMEM((4, ROWS, 128), BF16), pltpu.VMEM((512, 128), F32), pltpu.VMEM((512, 128), F32)]
    cells, wide = shape((4, 128, 128), BF16), shape((4, 128, 128), F32)
    state, ranks, recv, place, grid, table, weights, floor, spots = pl.pallas_call(
        begin,
        name="begin",
        out_shape=(
            cells,
            shape((4, 128), F32),
            wide,
            shape((4, 4, 128, 128), F32),
            shape((12, ROWS, 128), BF16),
            shape((24, 128), jnp.int32),
            shape((8, 128), F32),
            shape((4096, 128), F32),
            shape((12, 3, 24, 128), F32),
        ),
        in_specs=[FIXED, VMEM, VMEM, FIXED, FIXED] + [VMEM] * 4,
        out_specs=(VMEM,) * 9,
        scratch_shapes=work
        + sems
        + [pltpu.VMEM((4, 128, 128), BF16), pltpu.VMEM((2, 128, 128), BF16), pltpu.VMEM((2, 128, 128), BF16)]
        + [pltpu.SemaphoreType.DMA((3,))],
        compiler_params=pltpu.CompilerParams(collective_id=0, has_side_effects=True, vmem_limit_bytes=LIMIT),
    )(
        *(
            pltpu.with_memory_space_constraint(x, pltpu.HBM)
            for x in (
                latent.reshape(4, 128, 128),
                offset.transpose(0, 2, 1, 3),
                occupied.reshape(4, 128),
                w_send,
                w_recv,
                b_edge,
                w_disp,
                w_dist,
                pair_list.reshape(1, -1),
            )
        )
    )
    scratch = [
        pltpu.VMEM((4096, 128), F32),
        pltpu.VMEM((512, 128), F32),
        pltpu.VMEM((9 * 160, 128), F32),
        pltpu.VMEM((148 * 8, 128), F32),
        pltpu.VMEM((9, 4, 24, 128), F32),
        pltpu.VMEM((148 * 16, 128), F32),
        pltpu.VMEM((148 * 16, 128), F32),
        pltpu.VMEM((512, 128), F32),
        pltpu.SMEM((4, 27), jnp.int32),
        pltpu.SMEM((4,), jnp.int32),
    ]
    msg_in = pl.pallas_call(
        functools.partial(pairs, 0, False),
        name="pairs_0",
        out_shape=shape((512, 128), BF16),
        in_specs=[SMEM] + [VMEM] * 6,
        out_specs=VMEM,
        scratch_shapes=scratch,
        compiler_params=pltpu.CompilerParams(vmem_limit_bytes=LIMIT),
    )(table, grid, recv, place, weights, spots, floor)
    state, recv, grid, floor = pl.pallas_call(
        middle,
        name="middle",
        out_shape=(cells, wide, shape((12, ROWS, 128), BF16), shape((4096, 128), F32)),
        in_specs=[VMEM] * 13,
        out_specs=(VMEM,) * 4,
        scratch_shapes=work + sems,
        compiler_params=pltpu.CompilerParams(collective_id=1, has_side_effects=True, vmem_limit_bytes=LIMIT),
    )(state, msg_in, grid, place, w_send, w_recv, b_edge, w_disp, w_self, w_msg, b_node, w_out, gain)
    out = pl.pallas_call(
        functools.partial(pairs, 1, True),
        name="pairs_1",
        out_shape=cells,
        in_specs=[SMEM] + [VMEM] * 13,
        out_specs=VMEM,
        scratch_shapes=scratch,
        compiler_params=pltpu.CompilerParams(vmem_limit_bytes=LIMIT),
    )(table, grid, recv, place, weights, spots, floor, state, ranks, w_self, w_msg, b_node, w_out, gain)
    return out.reshape(latent.shape)


def solution(mesh):
    return jax.shard_map(
        per_device,
        mesh=mesh,
        in_specs=(
            P("len", "wid", None, None),
            P("len", "wid", None, None),
            P("len", "wid", None),
            P("len", "wid", None),
        )
        + (P(),) * 10,
        out_specs=P("len", "wid", None, None),
        check_vma=False,
    )
```

```python
import functools

import jax
import jax.numpy as jnp
from jax import lax
from jax.experimental import pallas as pl
from jax.experimental.pallas import tpu as pltpu
from jax.sharding import PartitionSpec as P

EPSILON = 1e-05
FAR = 64.0
F32 = jnp.float32
BF16 = jnp.bfloat16
ROWS = 144
LIMIT = 16 << 20
VMEM = pl.BlockSpec(memory_space=pltpu.VMEM)
FIXED = pl.BlockSpec(memory_space=pltpu.HBM)
SMEM = pl.BlockSpec(memory_space=pltpu.SMEM)


def iota(shape, dim):
    return lax.broadcasted_iota(jnp.int32, shape, dim)


def swap_lanes(x, step):
    if step == 64:
        return pltpu.roll(x, 64, 1)
    low = (iota(x.shape, 1) & step) == 0
    return jnp.where(low, pltpu.roll(x, 128 - step, 1), pltpu.roll(x, step, 1))


def pick_lanes(x, index):
    return jnp.take_along_axis(x, index, axis=1)


def split_row(row):
    index = 16 * iota((8, 128), 0) + (iota((8, 128), 1) & 15)
    return pick_lanes(jnp.broadcast_to(row, (8, 128)), index)


def split_rows(src, dst):
    lane = iota((8, 128), 1)
    for base in range(0, src.shape[0], 64):
        parts = [src[pl.ds(base + m, 8, stride=8), :] for m in range(8)]
        for bit in (4, 2, 1):
            step = 16 * bit
            low = (lane & step) == 0
            for m in range(8):
                if m & bit:
                    continue
                a, b = parts[m], parts[m + bit]
                parts[m] = jnp.where(low, a, pltpu.roll(b, step, 1))
                parts[m + bit] = jnp.where(low, pltpu.roll(a, 128 - step, 1), b)
        for q in range(8):
            dst[pl.ds(base + q, 8, stride=8), :] = parts[q]


def project_send(state, step, w_send, msg, flat, split):
    flat[...] = jnp.dot(state, w_send[step], preferred_element_type=F32)
    split_rows(flat, split)
    for cell in range(4):
        msg[cell, 0:128, :] = split[cell * 128 : cell * 128 + 128, :].astype(BF16)


def project_recv(state, step, w_recv, b_edge, w_disp, place, recv):
    r = jnp.dot(state, w_recv[step], preferred_element_type=F32) + b_edge[step : step + 1, :]
    r = r.astype(BF16).astype(F32)
    for cell in range(4):
        pull = sum(place[cell, k] * w_disp[k, step : step + 1, :] for k in range(3))
        recv[cell] = r[cell * 128 : cell * 128 + 128] - pull


def spread_recv(recv, floor):
    def some(group, _):
        for t in range(4):
            tile = group * 4 + t
            x = -recv[tile >> 4, pl.ds(pl.multiple_of((tile & 15) * 8, 8), 8), :]
            for q in range(8):
                floor[pl.ds(tile * 64 + q, 8, stride=8), :] = pick_lanes(x, 16 * q + (iota((8, 128), 1) & 15))
        return 0

    lax.fori_loop(0, 16, some, 0)


def peers():
    me_len, me_wid = lax.axis_index("len"), lax.axis_index("wid")
    count = lax.axis_size("wid")
    right, left = lax.rem(me_wid + 1, count), lax.rem(me_wid + count - 1, count)
    return me_len, me_wid, left, right


def greet():
    me_len, me_wid, left, right = peers()
    other = 1 - me_len
    barrier = pltpu.get_barrier_semaphore()
    for peer in ((me_len, left), (me_len, right), (other, me_wid), (other, left), (other, right)):
        pl.semaphore_signal(barrier, inc=1, device_id=peer, device_id_type=pl.DeviceIdType.MESH)


def send_all(msg, grid, rows, send_sem, recv_sem, own_sem):
    me_len, me_wid, left, right = peers()
    other = 1 - me_len
    edge = 1 - me_len
    pl.semaphore_wait(pltpu.get_barrier_semaphore(), 5)
    plan = (
        (pl.ds(0, 2), pl.ds(6, 2), (me_len, left)),
        (pl.ds(2, 2), pl.ds(4, 2), (me_len, right)),
        (pl.ds(edge, 1), pl.ds(11, 1), (other, left)),
        (pl.ds(2 + edge, 1), pl.ds(8, 1), (other, right)),
        (pl.ds(edge, 1), pl.ds(9, 1), (other, me_wid)),
        (pl.ds(2 + edge, 1), pl.ds(10, 1), (other, me_wid)),
    )
    copies = []
    for k, (src, dst, peer) in enumerate(plan):
        copy = pltpu.make_async_remote_copy(
            src_ref=msg.at[src, pl.ds(0, rows)],
            dst_ref=grid.at[dst, pl.ds(0, rows)],
            send_sem=send_sem.at[k],
            recv_sem=recv_sem.at[k],
            device_id=peer,
            device_id_type=pl.DeviceIdType.MESH,
        )
        copy.start()
        copies.append(copy)
    own = pltpu.make_async_copy(msg.at[:, pl.ds(0, rows)], grid.at[pl.ds(0, 4), pl.ds(0, rows)], own_sem)
    own.start()
    return copies + [own]


def begin(latent_in, offset, occupied, w_send_in, w_recv_in, b_edge, w_disp, w_dist, codes, *refs):
    state, ranks, recv, place, grid, table, push_out, floor, spots = refs[:9]
    msg, flat, split, send_sem, recv_sem, own_sem, latent, w_send, w_recv, load_sem = refs[9:]
    greet()
    loads = [
        pltpu.make_async_copy(src, dst, load_sem.at[k])
        for k, (src, dst) in enumerate(((latent_in, latent), (w_send_in, w_send), (w_recv_in, w_recv)))
    ]
    for load in loads:
        load.start()
    occ = occupied[...].astype(F32)
    total = jnp.sum(occ, axis=1, keepdims=True)
    line, lane = iota((128, 128), 0), iota((128, 128), 1)
    slot = line.astype(F32)
    same = (line == lane).astype(F32).astype(BF16)
    both = (((1,), (1,)), ((), ()))
    perms = [None] * 4
    for row in range(2):
        for col in range(2):
            given, cell = row * 2 + col, col * 2 + row
            held = occ[given : given + 1]
            key = (offset[row, 1, col : col + 1, :].astype(F32) + 2.0 * (1.0 - held)).astype(BF16)
            key_row = jnp.broadcast_to(key.astype(F32), (128, 128))
            key_col = lax.dot_general(same, key_row.astype(BF16), both, preferred_element_type=F32)
            ahead = (key_col < key_row) | ((key_col == key_row) & (line < lane))
            rank = jnp.sum(ahead.astype(F32), axis=0, keepdims=True)
            ranks[given : given + 1, :] = rank
            perm = (slot == rank).astype(F32).astype(BF16)
            perms[cell] = perm
            geo = [offset[row, k, col : col + 1, :].astype(F32) for k in range(3)]
            geo = jnp.concatenate(geo + [held, jnp.zeros((12, 128), F32)], axis=0).astype(BF16)
            moved = lax.dot_general(geo, perm, both, preferred_element_type=F32)
            msg[cell, 128:ROWS, :] = moved.astype(BF16)
    for load in loads:
        load.wait()
    for cell in range(4):
        given = (cell & 1) * 2 + (cell >> 1)
        state[cell] = jnp.dot(perms[cell], latent[given], preferred_element_type=F32).astype(BF16)
    project_send(state[...].reshape(512, 128), 0, w_send, msg, flat, split)
    copies = send_all(msg, grid, ROWS, send_sem, recv_sem, own_sem)
    for row in range(2):
        for col in range(2):
            given, cell = row * 2 + col, col * 2 + row
            full = slot < total[given : given + 1, :]
            for k in range(3):
                part = jnp.broadcast_to(offset[row, k, col : col + 1, :].astype(F32), (128, 128)).astype(BF16)
                spread = lax.dot_general(perms[cell], part, both, preferred_element_type=F32)
                place[cell, k] = jnp.where(full, spread, -FAR) if k == 2 else spread
            parts = [place[cell, k] for k in range(3)]
            place[cell, 3] = 1.0 - parts[0] * parts[0] - parts[1] * parts[1] - parts[2] * parts[2]
    project_recv(state[...].reshape(512, 128), 0, w_recv, b_edge, w_disp, place, recv)
    spread_recv(recv, floor)
    for step in range(2):
        for k in range(3):
            line_of = 4 * step + k
            push_out[line_of : line_of + 1, :] = w_disp[k, step : step + 1, :]
        push_out[4 * step + 3 : 4 * step + 4, :] = w_dist[step : step + 1, :]
    code = codes[...]
    valid = code >= 0
    code = jnp.maximum(code, 0)
    given = (code * 57) >> 9
    direction = code - given * 9
    up = ((direction * 11) >> 5) - 1
    side = direction - 3 * up - 4
    at_row, at_col = (given >> 1) + 1 + up, (given & 1) + 1 + side
    in_rows = (at_row == 1) | (at_row == 2)
    in_cols = (at_col == 1) | (at_col == 2)
    beyond = at_row == jnp.where(lax.axis_index("len") == 0, 3, 0)
    inner = (at_col - 1) * 2 + at_row - 1
    outer = jnp.where(in_rows, jnp.where(at_col == 3, 6, 4) + at_row - 1, 8 + at_col)
    width = codes.shape[1]
    table[17:18, 0:width] = jnp.where(valid & (in_rows | beyond), (given & 1) * 2 + (given >> 1), 4)
    table[18:19, 0:width] = jnp.where(in_rows & in_cols, inner, outer)
    table[19:20, 0:width] = up
    table[20:21, 0:width] = side

    wide_lane = iota((8, 128), 1)
    lower = wide_lane < 64
    edge_of = jnp.where(lower, 8 * (wide_lane & 15) + 7, 8 * (wide_lane & 15))
    edges = jnp.zeros((8, 128), F32)
    for cell in range(4):
        given = (cell & 1) * 2 + (cell >> 1)
        found = pick_lanes(jnp.broadcast_to(msg[cell, 128:ROWS, :].astype(F32)[1:2], (8, 128)), edge_of)
        found = jnp.where(lower & (edge_of.astype(F32) >= total[given : given + 1, :]), 2.0, found)
        edges = jnp.where(((wide_lane >> 4) & 3) == cell, found, edges)
    edges = edges[0:1]
    first_slot = (8 * iota((16, 128), 0)).astype(F32)

    def describe(cell, geo, held):
        count = jnp.sum(geo[3:4], axis=1, keepdims=True)
        for k in range(3):
            row = geo[k : k + 1]
            if k == 2:
                row = row + FAR * (1.0 - geo[3:4])
            row = jnp.broadcast_to(row, (8, 128))
            index = 8 * iota((8, 128), 0) + (wide_lane >> 4)
            places = jnp.concatenate([pick_lanes(row, index), pick_lanes(row, index + 64)], axis=0)
            spots[cell, k, 0:16, :] = places
            spots[cell, k, 16:24, :] = jnp.full((8, 128), FAR)
            if k == 1:
                begins = jnp.broadcast_to(places[:, 0:1], (16, 128))
                ends = jnp.broadcast_to(places[:, 127:128], (16, 128))
        begins = jnp.where(first_slot < count, begins, 4.0)
        ends = jnp.where(first_slot + 7.0 < count, ends, 4.0)
        hits = jnp.where(iota((16, 128), 1) < 64, (begins < edges).astype(F32), (ends <= edges).astype(F32))
        table[cell : cell + 1, :] = jnp.sum(hits, axis=0, keepdims=True).astype(jnp.int32)
        return jnp.where(wide_lane[0:1] == cell, count, held)

    held = jnp.zeros((1, 128), F32)
    for cell in range(4):
        held = describe(cell, msg[cell, 128:ROWS, :].astype(F32), held)
    for copy in copies:
        copy.wait()
    for cell in range(4, 12):
        held = describe(cell, grid[cell, 128:ROWS, :].astype(F32), held)
    table[16:17, :] = held.astype(jnp.int32)


def node_update(step, state, msg_in, w_self, w_msg, b_node, w_out, gain):
    h = state[...].reshape(512, 128)
    pre = (
        jnp.dot(h, w_self[step], preferred_element_type=F32)
        + jnp.dot(msg_in, w_msg[step], preferred_element_type=F32)
        + b_node[step : step + 1, :]
    )
    hidden = jnp.maximum(pre, 0.0).astype(BF16)
    y = jnp.dot(hidden, w_out[step], preferred_element_type=F32)
    center = jnp.mean(y, axis=-1, keepdims=True)
    spread = jnp.mean(jnp.square(y - center), axis=-1, keepdims=True)
    normed = (y - center) / jnp.sqrt(spread + EPSILON)
    return (h.astype(F32) + normed * gain[step : step + 1, :]).astype(BF16)


def middle(state, msg_in, before, place, w_send, w_recv, b_edge, w_disp, *refs):
    w_self, w_msg, b_node, w_out, gain = refs[:5]
    state_out, recv, grid, floor, msg, flat, split, send_sem, recv_sem, own_sem = refs[5:]
    greet()
    new = node_update(0, state, msg_in[...], w_self, w_msg, b_node, w_out, gain)
    state_out[...] = new.reshape(4, 128, 128)
    project_send(new, 1, w_send, msg, flat, split)
    copies = send_all(msg, grid, 128, send_sem, recv_sem, own_sem)
    project_recv(new, 1, w_recv, b_edge, w_disp, place, recv)
    spread_recv(recv, floor)
    for cell in range(12):
        grid[cell, 128:ROWS, :] = before[cell, 128:ROWS, :]
    for copy in copies:
        copy.wait()


def pairs(step, last, table, grid, recv, place, weights, spots, floor, *refs):
    if last:
        state, ranks, w_self, w_msg, b_node, w_out, gain, out = refs[:8]
        rest = refs[8:]
    else:
        (msg_in,) = refs[:1]
        rest = refs[1:]
    acc, csum, sent, queue, feats, far, close, incoming, plan, many = rest
    counts = [table[16, cell] for cell in range(4)]

    acc[...] = jnp.zeros_like(acc)
    csum[...] = jnp.zeros_like(csum)
    incoming[...] = jnp.zeros_like(incoming)

    push = [split_row(weights[4 * step + k : 4 * step + k + 1, :]) for k in range(3)]
    pull = split_row(weights[4 * step + 3 : 4 * step + 4, :])

    for cell in range(5):
        many[cell] = 0

    def enlist(p, _):
        cell = table[17, p]
        spot = many[cell]
        for k in range(3):
            plan[cell, 3 * spot + k] = table[18 + k, p]
        many[cell] = spot + 1
        return 0

    lax.fori_loop(0, 36, enlist, 0)

    def one_cell(cell, _):
        here, entries = table[16, cell], many[cell]

        def fill(q, _):
            source, up, side = (plan[cell, 3 * q + k] for k in range(3))
            shift = [jnp.full((1, 128), s.astype(F32)) for s in (up, side)]

            x, y, z = spots[source, 0] + shift[0], spots[source, 1] + shift[1], spots[source, 2]
            feats[q, 0], feats[q, 1], feats[q, 2] = x + x, y + y, z + z
            feats[q, 3] = -(x * x + y * y + z * z)

            for at in range(16):
                r = slice(at, at + 1)
                t = grid[source, at * 8 : at * 8 + 8, :].astype(F32) + pull
                sent[pl.ds(pl.multiple_of(q * 160 + at * 8, 8), 8), :] = (
                    t + x[r] * push[0] + y[r] * push[1] + z[r] * push[2]
                )
            return 0

        lax.fori_loop(0, entries, fill, 0)

        def block_of(tiles, tile):
            size = 8 * tiles
            start = pl.multiple_of(cell * 128 + tile * 8, 8)
            rows = [pl.ds(pl.multiple_of(tile * 8 + 8 * t, 8), 8) for t in range(tiles)]
            own = [[place[cell, k, rows[t], :] for k in range(4)] for t in range(tiles)]

            def measure(q, carry):
                front, weight = carry[0], carry[1:]
                source, side = plan[cell, 3 * q], plan[cell, 3 * q + 2]
                lines = (table[16, source] + 7) >> 3
                most = jnp.where(side == 1, table[source, cell * 16 + tile + tiles - 1], lines)
                least = jnp.where(side == -1, table[source, 64 + cell * 16 + tile], 0)
                span = jnp.maximum(most - least, 0)

                def some(b, weight):
                    weight = list(weight)
                    for r in range(4):
                        at, to = least + b * 4 + r, front + b * 4 + r
                        x, y, z, base = (feats[q, k, pl.ds(at, 1), :] for k in range(4))
                        take = pl.ds(pl.multiple_of(q * 160 + at * 8, 8), 8)
                        queue[pl.ds(pl.multiple_of(to * 8, 8), 8), :] = sent[take, :]
                        for t in range(tiles):
                            ox, oy, oz, mine = own[t]
                            d = (mine + base) + ox * x + oy * y + oz * z
                            c = jnp.maximum(d, 0.0)
                            c = c * c
                            put = pl.ds(pl.multiple_of(to * 16 + 8 * t, 8), 8)
                            far[put, :] = d
                            close[put, :] = c
                            weight[t] = weight[t] + c
                    return tuple(weight)

                weight = lax.fori_loop(0, (span + 3) >> 2, some, weight)
                return (front + span,) + tuple(weight)

            nothing = jnp.zeros((8, 128), F32)
            carry = lax.fori_loop(0, entries, measure, (jnp.int32(0),) + (nothing,) * tiles)
            front = carry[0]
            for t in range(tiles):
                csum[pl.ds(start + 8 * t, 8), :] = carry[1 + t]
            for r in range(3):
                queue[pl.ds(pl.multiple_of((front + r) * 8, 8), 8), :] = nothing
                for t in range(tiles):
                    far[pl.ds(pl.multiple_of((front + r) * 16 + 8 * t, 8), 8), :] = nothing
                    close[pl.ds(pl.multiple_of((front + r) * 16 + 8 * t, 8), 8), :] = nothing

            first = pl.multiple_of(start * 8, 64)
            nr = [floor[pl.ds(first + 8 * i, 8), :] for i in range(size)]

            def senders(b, carry):
                sums = list(carry)
                for r in range(4):
                    at = b * 4 + r
                    s = queue[pl.ds(pl.multiple_of(at * 8, 8), 8), :]
                    for i in range(size):
                        d = far[pl.ds(at * 16 + i, 1), :]
                        c = close[pl.ds(at * 16 + i, 1), :]
                        sums[i] = sums[i] + c * jnp.maximum(s - d * pull, nr[i])
                return tuple(sums)

            sums = lax.fori_loop(0, (front + 3) >> 2, senders, (nothing,) * size)
            for i in range(size):
                acc[pl.ds(first + 8 * i, 8), :] = sums[i]

        def pair_of_tiles(b, _):
            block_of(2, 2 * b)
            return 0

        def odd_tile(b, _):
            block_of(1, b)
            return 0

        tiles = (here + 7) >> 3
        lax.fori_loop(0, tiles >> 1, pair_of_tiles, 0)
        lax.fori_loop(tiles & ~1, tiles, odd_tile, 0)
        return 0

    lax.fori_loop(0, 4, one_cell, 0)

    for cell in range(4):

        def gather(group, _, cell=cell):
            lane = iota((8, 128), 1)
            for t in range(4):
                at = pl.multiple_of(group * 32 + 8 * t, 8)
                base = (cell * 128 + at) * 8
                parts = [acc[pl.ds(base + q, 8, stride=8), :] for q in range(8)]
                for bit in (4, 2, 1):
                    low = (lane & (16 * bit)) == 0
                    parts = [
                        jnp.where(low, parts[q], parts[q + bit])
                        + swap_lanes(jnp.where(low, parts[q + bit], parts[q]), 16 * bit)
                        for q in range(bit)
                    ]
                weight = jnp.sum(csum[pl.ds(cell * 128 + at, 8), :], axis=1, keepdims=True) * (1.0 / 16.0)
                incoming[pl.ds(cell * 128 + at, 8), :] = parts[0] + recv[cell, pl.ds(at, 8), :] * weight
            return 0

        lax.fori_loop(0, (counts[cell] + 31) >> 5, gather, 0)

    rounded = (incoming[...] * (8.0 / 128.0)).astype(BF16)
    if not last:
        msg_in[...] = rounded
        return
    new = node_update(step, state, rounded, w_self, w_msg, b_node, w_out, gain)
    slot = iota((128, 128), 0).astype(F32)
    for cell in range(4):
        given = (cell & 1) * 2 + (cell >> 1)
        perm = (slot == ranks[given : given + 1, :]).astype(F32).astype(BF16)
        here = new[cell * 128 : cell * 128 + 128]
        back = lax.dot_general(perm, here, (((0,), (0,)), ((), ())), preferred_element_type=F32)
        out[given] = back.astype(BF16)


def per_device(
    latent, offset, occupied, pair_list, w_send, w_recv, b_edge, w_disp, w_dist, w_self, w_msg, b_node, w_out, gain
):
    shape = jax.ShapeDtypeStruct
    w_disp = w_disp.transpose(1, 0, 2)
    sems = [pltpu.SemaphoreType.DMA((6,)), pltpu.SemaphoreType.DMA((6,)), pltpu.SemaphoreType.DMA]
    work = [pltpu.VMEM((4, ROWS, 128), BF16), pltpu.VMEM((512, 128), F32), pltpu.VMEM((512, 128), F32)]
    cells, wide = shape((4, 128, 128), BF16), shape((4, 128, 128), F32)
    state, ranks, recv, place, grid, table, weights, floor, spots = pl.pallas_call(
        begin,
        name="begin",
        out_shape=(
            cells,
            shape((4, 128), F32),
            wide,
            shape((4, 4, 128, 128), F32),
            shape((12, ROWS, 128), BF16),
            shape((24, 128), jnp.int32),
            shape((8, 128), F32),
            shape((4096, 128), F32),
            shape((12, 3, 24, 128), F32),
        ),
        in_specs=[FIXED, VMEM, VMEM, FIXED, FIXED] + [VMEM] * 4,
        out_specs=(VMEM,) * 9,
        scratch_shapes=work
        + sems
        + [pltpu.VMEM((4, 128, 128), BF16), pltpu.VMEM((2, 128, 128), BF16), pltpu.VMEM((2, 128, 128), BF16)]
        + [pltpu.SemaphoreType.DMA((3,))],
        compiler_params=pltpu.CompilerParams(collective_id=0, has_side_effects=True, vmem_limit_bytes=LIMIT),
    )(
        *(
            pltpu.with_memory_space_constraint(x, pltpu.HBM)
            for x in (
                latent.reshape(4, 128, 128),
                offset.transpose(0, 2, 1, 3),
                occupied.reshape(4, 128),
                w_send,
                w_recv,
                b_edge,
                w_disp,
                w_dist,
                pair_list.reshape(1, -1),
            )
        )
    )
    scratch = [
        pltpu.VMEM((4096, 128), F32),
        pltpu.VMEM((512, 128), F32),
        pltpu.VMEM((9 * 160, 128), F32),
        pltpu.VMEM((148 * 8, 128), F32),
        pltpu.VMEM((9, 4, 24, 128), F32),
        pltpu.VMEM((148 * 16, 128), F32),
        pltpu.VMEM((148 * 16, 128), F32),
        pltpu.VMEM((512, 128), F32),
        pltpu.SMEM((5, 108), jnp.int32),
        pltpu.SMEM((5,), jnp.int32),
    ]
    msg_in = pl.pallas_call(
        functools.partial(pairs, 0, False),
        name="pairs_0",
        out_shape=shape((512, 128), BF16),
        in_specs=[SMEM] + [VMEM] * 6,
        out_specs=VMEM,
        scratch_shapes=scratch,
        compiler_params=pltpu.CompilerParams(vmem_limit_bytes=LIMIT),
    )(table, grid, recv, place, weights, spots, floor)
    state, recv, grid, floor = pl.pallas_call(
        middle,
        name="middle",
        out_shape=(cells, wide, shape((12, ROWS, 128), BF16), shape((4096, 128), F32)),
        in_specs=[VMEM] * 13,
        out_specs=(VMEM,) * 4,
        scratch_shapes=work + sems,
        compiler_params=pltpu.CompilerParams(collective_id=1, has_side_effects=True, vmem_limit_bytes=LIMIT),
    )(state, msg_in, grid, place, w_send, w_recv, b_edge, w_disp, w_self, w_msg, b_node, w_out, gain)
    out = pl.pallas_call(
        functools.partial(pairs, 1, True),
        name="pairs_1",
        out_shape=cells,
        in_specs=[SMEM] + [VMEM] * 13,
        out_specs=VMEM,
        scratch_shapes=scratch,
        compiler_params=pltpu.CompilerParams(vmem_limit_bytes=LIMIT),
    )(table, grid, recv, place, weights, spots, floor, state, ranks, w_self, w_msg, b_node, w_out, gain)
    return out.reshape(latent.shape)


def solution(mesh):
    return jax.shard_map(
        per_device,
        mesh=mesh,
        in_specs=(
            P("len", "wid", None, None),
            P("len", "wid", None, None),
            P("len", "wid", None),
            P("len", "wid", None),
        )
        + (P(),) * 10,
        out_specs=P("len", "wid", None, None),
        check_vma=False,
    )
```
